256 devices in a mesh: seq: 64 (over z, y, core), dp: 4 (over x).
Axes of the slice: x: 4, y: 4, z: 8, core: 2. Of those that a mesh axis runs over, the one named last changes fastest.
Arguments:
- inputs: bfloat16 [4, 16384, 512], P('dp', 'seq'), may hold values from -16 to 16
- write_vecs: bfloat16 [4, 16384, 128], P('dp', 'seq'), may hold values from -6 to 6
- read_vecs: bfloat16 [4, 16384, 128], P('dp', 'seq'), may hold values from -0.5 to 0.5
- dt_code: int32 [4, 8, 16384], P('dp', None, 'seq'), may hold values from 1 to 81920
- a_rate: float32 [8], replicated, may hold values from 0.4 to 682.6667
- w_out: bfloat16 [512, 2560], replicated, may hold values from -0.125 to 0.125
- grad_out: bfloat16 [4, 16384, 2560], P('dp', 'seq'), may hold values from -0.59765625 to 0.59765625
Outputs:
- outputs: bfloat16 [4, 16384, 512], P('dp', 'seq')
- grad_inputs: bfloat16 [4, 16384, 512], P('dp', 'seq')
- grad_write: bfloat16 [4, 16384, 128], P('dp', 'seq')
- grad_read: bfloat16 [4, 16384, 128], P('dp', 'seq')
- grad_w_out: float32 [512, 2560], P('seq')
The draws below stay inside these ranges and needn't reach their ends.
All inputs are finite; a program needn't handle non-finite values.
Results may differ from the reference program's by a relative error of at most 0.0055.
Values sent between devices are 32-bit elements; how exact they have to be, the bound alone decides.
No kernel may reach another device: no remote copies, remote signals or barrier semaphores. Data moves between devices by JAX's collectives and lax.ppermute only.
A program may use at most 128 MiB of HBM per device.

```python
import jax
import jax.numpy as jnp
from jax import lax

D_MODEL = 2560
HEAD_DIM = 64
STATE = 128
LOCAL_HEADS = 8
GROUP = 128
TOK_DEV = 256
SEQUENCE_LENGTH = 16384
BATCH_SEQUENCES = 4
CHANNELS = 512


def draw_dt_code(key, part):
    first_key, second_key, random_key_three = jax.random.split(jax.random.fold_in(key, 11), 3)
    blocks = SEQUENCE_LENGTH // TOK_DEV
    levels = jax.random.randint(first_key, (BATCH_SEQUENCES, LOCAL_HEADS, blocks, 1), 4, 13)
    random_bits = jax.random.randint(second_key, (BATCH_SEQUENCES, LOCAL_HEADS, blocks, TOK_DEV), 0, 1 << 20)
    label_values = (1 + random_bits % (2 * levels - 1)).reshape(BATCH_SEQUENCES, LOCAL_HEADS, SEQUENCE_LENGTH)
    spike_start = jax.random.randint(random_key_three, (BATCH_SEQUENCES, LOCAL_HEADS, 2, 1), 0, SEQUENCE_LENGTH)
    token_positions = jnp.arange(SEQUENCE_LENGTH, dtype=jnp.int32)[None, None, None, :]
    spike_spans = jnp.any(token_positions == spike_start, axis=2)
    return jnp.where(spike_spans, 5 * SEQUENCE_LENGTH, label_values).astype(jnp.int32)


def draw_a_rate(key, part):
    first_key, second_key, random_key_three = jax.random.split(jax.random.fold_in(key, 23), 3)
    order = jax.random.permutation(first_key, LOCAL_HEADS)
    fast_count = jax.random.randint(random_key_three, (), LOCAL_HEADS // 4, 3 * LOCAL_HEADS // 4 + 1)
    spread = jax.random.uniform(second_key, (LOCAL_HEADS,), jnp.float32)
    fast = order < fast_count
    slow_rate = 0.4 * jnp.exp(spread * jnp.log(2.5))
    fast_rate = SEQUENCE_LENGTH * jnp.exp(jnp.log(1.0 / 64.0) + spread * jnp.log(64.0 / 24.0))
    return jnp.where(fast, fast_rate, slow_rate).astype(jnp.float32)


def strengthened(array, key, source, target, blocks, factor):
    owner, partner = [(jnp.arange(array.shape[axis_at]) // (array.shape[axis_at] // blocks)).reshape([-1 if axis == axis_at else 1 for axis in range(array.ndim)]) for axis_at in (source, target)]
    chosen = jax.random.permutation(key, blocks)[partner]
    strong = (owner == chosen) | (owner == (partner + blocks // 2) % blocks)
    return jnp.where(strong, factor * array, array)


def steps_of(stream_key, dims, shards, low, top_value):
    loudness, own = 1.0, jax.random.fold_in(stream_key, 6)
    for dim, blocks in shards:
        steps = jnp.exp(jax.random.uniform(jax.random.fold_in(own, dim), (blocks,), jnp.float32, low / len(shards), top_value / len(shards)))
        loudness = loudness * jnp.repeat(steps, dims[dim] // blocks).reshape([-1 if axis == dim else 1 for axis in range(len(dims))])
    return loudness


def centred(own_key, shape, scale, bound, shards=(), kind=jnp.bfloat16):
    factor_of = steps_of(own_key, shape, shards, -0.22, 0.18) if shards else 1.0
    result = jax.random.normal(own_key, shape, jnp.float32) * scale * factor_of
    return jnp.minimum(jnp.maximum(result, -bound), bound).astype(kind)


def heavy_noise(own_key, shape, scale, most, cuts, heavy, kind=jnp.bfloat16):
    values = scale * jax.random.normal(own_key, shape, jnp.float32)
    if cuts:
        values = values * steps_of(own_key, shape, cuts, -0.22, 0.18)
    return jnp.clip(strengthened(values, jax.random.fold_in(own_key, 3), *heavy), -most, most).astype(kind)


def setup_inputs(seed: int = 0) -> dict:
    key_of = jax.random.split(jax.random.key(seed), 8)
    inputs = heavy_noise(key_of[0], (BATCH_SEQUENCES, SEQUENCE_LENGTH, CHANNELS), 1.0, 16.0, ((0, 4), (1, 64)), (1, 2, 64, 4.0))
    write_vecs = centred(key_of[1], (BATCH_SEQUENCES, SEQUENCE_LENGTH, STATE), 1.0, 6.0, ((0, 4), (1, 64)))
    read_vecs = centred(key_of[2], (BATCH_SEQUENCES, SEQUENCE_LENGTH, STATE), STATE ** -0.5, 0.5, ((0, 4), (1, 64)))
    dt_code = draw_dt_code(jax.random.fold_in(key_of[7], 71), 0)
    a_rate = draw_a_rate(jax.random.fold_in(key_of[7], 71), 0)
    w_out = centred(key_of[5], (CHANNELS, D_MODEL), D_MODEL ** -0.5, 0.125)
    grad_out = centred(key_of[6], (BATCH_SEQUENCES, SEQUENCE_LENGTH, D_MODEL), 0.1, 0.59765625, ((0, 4), (1, 64)))
    return {"inputs": inputs, "write_vecs": write_vecs, "read_vecs": read_vecs, "dt_code": dt_code, "a_rate": a_rate, "w_out": w_out, "grad_out": grad_out}


highest = lax.Precision.HIGHEST

def group_step(state, pieces):
    x_group, b_group, c_group, decay_group = pieces
    cum_decay = jnp.cumsum(decay_group, axis=1)
    rows_at = lax.broadcasted_iota(jnp.int32, (GROUP, GROUP), 0)
    cols_at = lax.broadcasted_iota(jnp.int32, (GROUP, GROUP), 1)
    lower_tri = rows_at >= cols_at
    spread = cum_decay[:, :, None] - cum_decay[:, None, :]
    decay_mask = jnp.exp(jnp.where(lower_tri[None], spread, -jnp.inf))
    scores = jnp.einsum('in,jn->ij', c_group, b_group, precision=highest)
    y_intra = jnp.einsum('hij,jhp->ihp', decay_mask * scores[None], x_group, precision=highest)
    y_inter = jnp.einsum('in,hpn->ihp', c_group, state, precision=highest) * jnp.exp(cum_decay).T[:, :, None]
    group_last = cum_decay[:, -1]
    tail_decay = jnp.exp(group_last[:, None] - cum_decay)
    fresh = jnp.einsum('jhp,jn->hpn', x_group * tail_decay.T[:, :, None], b_group, precision=highest)
    return (jnp.exp(group_last)[:, None, None] * state + fresh, y_intra + y_inter)

def sequence_forward(weighted, write_rows, read_rows, log_decay):
    blocks = SEQUENCE_LENGTH // GROUP
    pieces = (weighted.reshape(blocks, GROUP, LOCAL_HEADS, HEAD_DIM), write_rows.reshape(blocks, GROUP, STATE), read_rows.reshape(blocks, GROUP, STATE), log_decay.reshape(LOCAL_HEADS, blocks, GROUP).transpose(1, 0, 2))
    start = jnp.zeros((LOCAL_HEADS, HEAD_DIM, STATE), jnp.float32)
    final, results = lax.scan(group_step, start, pieces)
    return results.reshape(SEQUENCE_LENGTH, LOCAL_HEADS, HEAD_DIM)

def reference(inputs, write_vecs, read_vecs, dt_code, a_rate, w_out, grad_out):
    decay_rate = a_rate / (8.0 * SEQUENCE_LENGTH)
    log_decay = -(decay_rate[None, :, None] * dt_code.astype(jnp.float32))
    weight = jnp.sqrt(-jnp.expm1(2.0 * log_decay))
    gate_rows = jnp.transpose(weight, (0, 2, 1))[..., None]
    weighted = inputs.astype(jnp.float32).reshape(BATCH_SEQUENCES, SEQUENCE_LENGTH, LOCAL_HEADS, HEAD_DIM) * gate_rows
    write_rows = write_vecs.astype(jnp.float32)
    read_rows = read_vecs.astype(jnp.float32)

    def forward(weighted_in, write_in, read_in):
        return jax.vmap(sequence_forward)(weighted_in, write_in, read_in, log_decay)
    y_full, pullback = jax.vjp(forward, weighted, write_rows, read_rows)
    outputs = y_full.reshape(BATCH_SEQUENCES, SEQUENCE_LENGTH, CHANNELS).astype(jnp.bfloat16)
    flat_grad = grad_out.reshape(BATCH_SEQUENCES * SEQUENCE_LENGTH, D_MODEL)
    grad_y = jnp.dot(flat_grad, w_out.T, preferred_element_type=jnp.float32).astype(jnp.bfloat16)
    grad_w_out = jnp.dot(outputs.reshape(BATCH_SEQUENCES * SEQUENCE_LENGTH, CHANNELS).T, flat_grad, preferred_element_type=jnp.float32)
    grad_weighted, grad_write, grad_read = pullback(grad_y.astype(jnp.float32).reshape(BATCH_SEQUENCES, SEQUENCE_LENGTH, LOCAL_HEADS, HEAD_DIM))
    grad_inputs = (grad_weighted * gate_rows).reshape(BATCH_SEQUENCES, SEQUENCE_LENGTH, CHANNELS).astype(jnp.bfloat16)
    return (outputs, grad_inputs, grad_write.astype(jnp.bfloat16), grad_read.astype(jnp.bfloat16), grad_w_out)
```

```python
import jax
import jax.numpy as jnp
from jax import lax
from jax.experimental import pallas as pl
from jax.experimental.pallas import tpu as pltpu
from jax.sharding import PartitionSpec as P

HEAD_DIM = 64
STATE = 128
HEADS = 8
TOK = 256
CH = HEADS * HEAD_DIM
D = 2560
NX, NY, NZ = 4, 4, 8
CHIPS = NY * NZ
PIECE = CH // CHIPS
BLK = D // NX
BOTH = ("seq", "dp")

f32, bf16 = jnp.float32, jnp.bfloat16
HI = lax.Precision.HIGHEST
NT = (((1,), (1,)), ((), ()))
TN = (((0,), (0,)), ((), ()))
NN = (((1,), (0,)), ((), ()))


def mm(a, b, dims):
    return lax.dot_general(a, b, dims, preferred_element_type=f32)


def permute(v, target):
    pairs = []
    for z in range(NZ):
        for y in range(NY):
            for c in range(2):
                for x in range(NX):
                    tz, ty, tc, tx = target(z, y, c, x)
                    src = ((z * NY + y) * 2 + c) * NX + x
                    dst = ((tz * NY + ty) * 2 + tc) * NX + tx
                    pairs.append((src, dst))
    return lax.ppermute(v, BOTH, pairs)


def swap_core(z, y, c, x):
    return z, y, 1 - c, x


def first_axis(k):
    return lambda z, y, c, x: (z, y, c, (x + k) % NX) if c == 0 else (z, (y + k) % NY, c, x)


def second_axis(k):
    return lambda z, y, c, x: (z, (y + k) % NY, c, x) if c == 0 else (z, y, c, (x + k) % NX)


def x_axis(k):
    return lambda z, y, c, x: (z, y, c, (x + k) % NX)


def rate_lanes(rate_ref, width):
    lane = lax.broadcasted_iota(jnp.int32, (1, width), 1) // (width // HEADS)
    rates = jnp.zeros((1, width), f32)
    for h in range(HEADS):
        rates = jnp.where(lane == h, rate_ref[h] * (1.0 / (8.0 * TOK * 64)), rates)
    return rates


def signed_tri():
    t = lax.broadcasted_iota(jnp.int32, (TOK, TOK), 0)
    s = lax.broadcasted_iota(jnp.int32, (TOK, TOK), 1)
    half = TOK // 2
    plus = (s >= half) & (s <= t)
    minus = (s < half) & (s > t)
    return jnp.where(plus, 1.0, jnp.where(minus, -1.0, 0.0)).astype(f32)


def gate(v):
    s = 1.0 - v * (1.0 / 8.0)
    for n in (7.0, 6.0, 5.0, 4.0, 3.0, 2.0):
        s = 1.0 - v * (1.0 / n) * s
    return jnp.sqrt(jnp.where(v < 0.25, v * s, 1.0 - jnp.exp(-v)))


def local_states(pos_ref, rate_ref, x_ref, b_ref, c_ref, dt_ref, w_ref, g_ref,
                 keep_ref, send_ref, tot_ref, gy_ref, gyd_ref, xw_ref, xt_ref, cum_ref):
    dt = dt_ref[...].astype(f32)
    dt_lanes = jnp.broadcast_to(dt[:, None, :], (HEADS, HEAD_DIM, TOK)).reshape(CH, TOK)
    cum = lax.dot_general(signed_tri(), dt_lanes, NT, precision=HI, preferred_element_type=f32)
    cum_ref[...] = cum
    steps = cum - pltpu.roll(cum, 1, 0)
    row = lax.broadcasted_iota(jnp.int32, (TOK, CH), 0)
    ones = jnp.ones((8, TOK // 2), f32)
    start = -lax.dot_general(ones, dt_lanes[:, : TOK // 2], NT, precision=HI, preferred_element_type=f32)[:1]
    steps = jnp.where(row == 0, cum - start, steps)
    rate = rate_lanes(rate_ref, CH)
    last = cum[TOK - 1:]
    xw = x_ref[...].astype(f32) * gate(steps * (2.0 * rate))
    xw_ref[...] = xw.astype(bf16)
    xt = (xw * jnp.exp((cum - last) * rate)).astype(bf16)
    xt_ref[...] = xt
    own = mm(xt, b_ref[...], TN)
    gy = mm(g_ref[...], w_ref[...], NT).astype(bf16)
    gy_ref[...] = gy
    gyd = (gy.astype(f32) * jnp.exp((start - cum) * rate)).astype(bf16)
    gyd_ref[...] = gyd
    adj = mm(gyd, c_ref[...], TN)
    total = jnp.sum(dt, axis=1, keepdims=True)
    head = lax.broadcasted_iota(jnp.int32, (HEADS, 1), 0)
    rate_col = jnp.zeros((HEADS, 1), f32)
    for h in range(HEADS):
        rate_col = jnp.where(head == h, rate_ref[h] * (1.0 / (8.0 * TOK * 64)), rate_col)
    tot = jnp.broadcast_to(-(total * rate_col), (HEADS, STATE))
    tot_ref[...] = tot
    send_ref[CH:, :] = tot
    core = pos_ref[2]

    @pl.when(core == 0)
    def _():
        keep_ref[...] = own
        send_ref[:CH, :] = adj

    @pl.when(core == 1)
    def _():
        keep_ref[...] = adj
        send_ref[:CH, :] = own


def per_head(rows):
    return jnp.broadcast_to(rows[:, None, :], (HEADS, HEAD_DIM, STATE)).reshape(CH, STATE)


def chip_states(keep_ref, recv_ref, tot_ref, out_ref):
    tot2 = recv_ref[CH:, :]
    chip = keep_ref[...] * per_head(jnp.exp(tot2)) + recv_ref[:CH, :]
    out_ref[:, :PIECE, :] = chip.reshape(CHIPS, PIECE, STATE)
    tots = (tot2 + tot_ref[...])[:, None, None, :]
    tots = jnp.broadcast_to(tots, (HEADS, CHIPS // HEADS, 8, STATE))
    out_ref[:, PIECE:, :] = tots.reshape(CHIPS, 8, STATE)


def scan_chips(pos_ref, in_ref, out_ref):
    core = pos_ref[2]

    def run(order):
        acc = jnp.zeros((PIECE, STATE), f32)
        for k in order:
            out_ref[k] = acc
            acc = acc * jnp.exp(in_ref[k, PIECE:PIECE + 1, :]) + in_ref[k, :PIECE, :]

    @pl.when(core == 0)
    def _():
        run(range(CHIPS))

    @pl.when(core == 1)
    def _():
        run(range(CHIPS - 1, -1, -1))


def core_states(carry_ref, keep_ref, tot_ref, out_ref):
    out_ref[...] = carry_ref[...] * per_head(jnp.exp(tot_ref[...])) + keep_ref[...]


def intra(rate_ref, dt_ref, cum_ref, b_ref, c_ref, gy_ref, xw_ref,
          y_ref, gin_ref, wt_ref, hd_ref, gr_ref, gw_ref):
    dt = dt_ref[...].astype(f32)
    tri = signed_tri()
    cum_rows = lax.dot_general(dt, tri, NT, precision=HI, preferred_element_type=f32)
    ones = jnp.ones((8, TOK), f32)
    rate = rate_lanes(rate_ref, CH)
    cum = cum_ref[...]
    i = lax.broadcasted_iota(jnp.int32, (TOK, TOK), 0)
    j = lax.broadcasted_iota(jnp.int32, (TOK, TOK), 1)
    lower = i >= j
    b = b_ref[...]
    c = c_ref[...]
    scores = mm(c, b, NT)
    pairs = jnp.zeros((TOK, TOK), f32)
    for h in range(HEADS):
        lanes = slice(h * HEAD_DIM, (h + 1) * HEAD_DIM)
        r = rate_ref[h] * (1.0 / (8.0 * TOK * 64))
        gap = cum_rows[h:h + 1, :] - cum[:, h * HEAD_DIM:h * HEAD_DIM + 1]
        mask = jnp.exp(jnp.where(lower, gap * r, -jnp.inf))
        mixed = (mask * scores).astype(bf16)
        xw = xw_ref[:, lanes]
        gy = gy_ref[:, lanes]
        y_ref[:, lanes] = mm(mixed, xw, NN)
        gin_ref[:, lanes] = mm(mixed, gy, TN)
        pairs = pairs + mask * mm(gy, xw, NT)
    pairs = pairs.astype(bf16)
    gr_ref[...] = mm(pairs, b, NN)
    gw_ref[...] = mm(pairs, c, TN)
    row = lax.broadcasted_iota(jnp.int32, (TOK, CH), 0)
    dt_lanes = jnp.broadcast_to(dt[:, None, :], (HEADS, HEAD_DIM, TOK)).reshape(CH, TOK)
    start = -lax.dot_general(ones[:, : TOK // 2], dt_lanes[:, : TOK // 2], NT, precision=HI,
                             preferred_element_type=f32)[:1]
    steps = jnp.where(row == 0, cum - start, cum - pltpu.roll(cum, 1, 0))
    w = gate(steps * (2.0 * rate))
    gin_ref[...] = gin_ref[...] * w
    wt_ref[...] = w * jnp.exp((cum - cum[TOK - 1:]) * rate)
    hd_ref[...] = jnp.exp((start - cum) * rate)


def select_rows(core, y_at):
    row = lax.broadcasted_iota(jnp.int32, (CH // 2, CH), 0)
    lane = lax.broadcasted_iota(jnp.int32, (CH // 2, CH), 1)
    y = (y_at + row // 64) % NY
    z = (row // 8) % NZ
    return jnp.where(lane == ((z * NY + y) * 2 + core) * 8 + row % 8, 1.0, 0.0).astype(bf16)


def forward_out(pos_ref, carry_ref, recv_ref, c_ref, y_ref, hd_ref, out_ref, mine_ref, other_ref):
    y_at, core = pos_ref[1], pos_ref[2]
    state = jnp.where(core == 0, carry_ref[...], recv_ref[...]).astype(bf16)
    out = (y_ref[...] + hd_ref[...] * mm(c_ref[...], state, NT)).astype(bf16)
    out_ref[...] = out
    mine_ref[...] = mm(select_rows(core, y_at), out, NT).astype(bf16)
    other_ref[...] = mm(select_rows(1 - core, y_at), out, NT)


def partial_grad(pos_ref, mine_ref, peer_ref, g_ref, gp_ref, s0_ref, s1_ref, s2_ref, s3_ref):
    core, x_at = pos_ref[2], pos_ref[3]
    outs = (s0_ref, s1_ref, s2_ref, s3_ref)
    mine = mine_ref[...]
    peer = peer_ref[...].astype(bf16)
    for xr in range(NX):
        at = pl.multiple_of(((x_at + xr) % NX) * BLK, 128)
        tile = mm(mine, g_ref[:, pl.ds(at, BLK)], NN)
        tile = tile + mm(peer, gp_ref[:, pl.ds(at, BLK)].astype(bf16), NN)

        @pl.when(core == 0)
        def _():
            for yr in range(NY):
                outs[xr][yr] = tile[yr * 64:(yr + 1) * 64]

        @pl.when(core == 1)
        def _():
            for yr in range(NY):
                outs[yr][xr] = tile[yr * 64:(yr + 1) * 64]


def other_grads(pos_ref, carry_ref, recv_ref, b_ref, gin_ref, wt_ref, gyd_ref, xt_ref, gr_ref, gw_ref,
                gi_ref, gwr_ref, grd_ref):
    core = pos_ref[2]
    carry, recv = carry_ref[...], recv_ref[...]
    state = jnp.where(core == 0, carry, recv).astype(bf16)
    adj = jnp.where(core == 0, recv, carry).astype(bf16)
    gi_ref[...] = (gin_ref[...] + wt_ref[...] * mm(b_ref[...], adj, NT)).astype(bf16)
    grd_ref[...] = (gr_ref[...] + mm(gyd_ref[...], state, NN)).astype(bf16)
    gwr_ref[...] = (gw_ref[...] + mm(xt_ref[...], adj, NN)).astype(bf16)


def place(pos_ref, r0_ref, r1_ref, r2_ref, r3_ref, out_ref):
    x_at = pos_ref[3]
    for k, ref in enumerate((r0_ref, r1_ref, r2_ref, r3_ref)):
        at = pl.multiple_of(((x_at + NX - k) % NX) * BLK, 128)
        out_ref[:, pl.ds(at, BLK)] = ref[...]


def call(body, outs, scalars, *args, flops=0):
    specs = [pl.BlockSpec(memory_space=pltpu.SMEM)] * scalars
    specs += [pl.BlockSpec(memory_space=pltpu.VMEM)] * (len(args) - scalars)
    shapes = [jax.ShapeDtypeStruct(s, d) for s, d in outs]
    moved = sum(a.size * a.dtype.itemsize for a in args) + sum(s.size * s.dtype.itemsize for s in shapes)
    got = pl.pallas_call(
        body,
        out_shape=shapes,
        in_specs=specs,
        out_specs=[pl.BlockSpec(memory_space=pltpu.VMEM)] * len(shapes),
        cost_estimate=pl.CostEstimate(flops=flops, bytes_accessed=moved, transcendentals=0),
        compiler_params=pltpu.CompilerParams(vmem_limit_bytes=48 << 20),
        name=body.__name__,
    )(*args)
    return got if len(got) > 1 else got[0]


def shards(inputs, write_vecs, read_vecs, dt_code, a_rate, w_out, grad_out):
    place_seq = lax.axis_index("seq")
    pos = jnp.stack([place_seq // 8, (place_seq // 2) % NY, place_seq % 2, lax.axis_index("dp")]).astype(jnp.int32)
    x, b, c, dt, g = inputs[0], write_vecs[0], read_vecs[0], dt_code[0], grad_out[0]
    chips = [[q * 2 + core for q in range(CHIPS)] for core in range(2)]
    depth = [[(z * NY + y) * 2 + core for z in range(NZ)] for y in range(NY) for core in range(2)]

    keep, send, tot, gy, gyd, xw, xt, cum = call(
        local_states,
        [((CH, STATE), f32), ((CH + 8, STATE), f32), ((HEADS, STATE), f32), ((TOK, CH), bf16), ((TOK, CH), bf16),
         ((TOK, CH), bf16), ((TOK, CH), bf16), ((TOK, CH), f32)],
        2, pos, a_rate, x, b, c, dt, w_out, g, flops=2 * TOK * D * CH)
    recv = permute(send, swap_core)
    chip = call(chip_states, [((CHIPS, PIECE + 8, STATE), f32)], 0, keep, recv, tot)
    pieces = lax.all_to_all(chip, "seq", 0, 0, axis_index_groups=chips, tiled=True)
    scanned = call(scan_chips, [((CHIPS, PIECE, STATE), f32)], 1, pos, pieces)
    carry = lax.all_to_all(scanned, "seq", 0, 0, axis_index_groups=chips, tiled=True).reshape(CH, STATE)
    recv2 = permute(call(core_states, [((CH, STATE), f32)], 0, carry, keep, tot), swap_core)

    g_peer = permute(g.astype(f32), swap_core)
    y_in, gin, wt, hd, gr, gw = call(
        intra,
        [((TOK, CH), f32), ((TOK, CH), f32), ((TOK, CH), f32), ((TOK, CH), f32), ((TOK, STATE), f32),
         ((TOK, STATE), f32)],
        1, a_rate, dt, cum, b, c, gy, xw, flops=2 * TOK * TOK * CH * 3)

    out, mine, other = call(
        forward_out, [((TOK, CH), bf16), ((CH // 2, TOK), bf16), ((CH // 2, TOK), f32)],
        1, pos, carry, recv2, c, y_in, hd, flops=2 * TOK * CH * 768)
    peer = permute(other, swap_core)
    tile = ((NY, 64, BLK), f32)
    s = call(partial_grad, [tile] * 4, 1, pos, mine, peer, g, g_peer, flops=2 * TOK * D * CH)
    s = s[0] + permute(s[2], first_axis(2)) + permute(s[1], first_axis(1)) + permute(s[3], first_axis(3))
    s = s[0] + permute(s[2], second_axis(2)) + permute(s[1], second_axis(1)) + permute(s[3], second_axis(3))
    s = lax.all_to_all(s.reshape(NZ, 8, BLK), "seq", 0, 0, axis_index_groups=depth, tiled=True)
    s = jnp.sum(s, axis=0)
    grad_w_out = call(place, [((8, D), f32)], 1, pos, s, permute(s, x_axis(1)), permute(s, x_axis(2)),
                      permute(s, x_axis(3)))
    gi, gwr, grd = call(
        other_grads, [((TOK, CH), bf16), ((TOK, STATE), bf16), ((TOK, STATE), bf16)],
        1, pos, carry, recv2, b, gin, wt, gyd, xt, gr, gw, flops=2 * TOK * CH * STATE * 3)
    return out[None], gi[None], gwr[None], grd[None], grad_w_out


def solution(mesh):
    rows = P("dp", "seq", None)
    return jax.shard_map(
        shards,
        mesh=mesh,
        in_specs=(rows, rows, rows, P("dp", None, "seq"), P(), P(), rows),
        out_specs=(rows, rows, rows, rows, P("seq", None)),
        check_vma=False,
    )
```

```python
import jax
import jax.numpy as jnp
from jax import lax
from jax.experimental import pallas as pl
from jax.experimental.pallas import tpu as pltpu
from jax.sharding import PartitionSpec as P

HEAD_DIM = 64
STATE = 128
HEADS = 8
TOK = 256
CH = HEADS * HEAD_DIM
D = 2560
NX, NY, NZ = 4, 4, 8
CHIPS = NY * NZ
HALF = CH // 2
PIECE = HALF // CHIPS
BLK = D // NX
BOTH = ("seq", "dp")

f32, bf16 = jnp.float32, jnp.bfloat16
RATE_UNIT = 1.0 / (8.0 * TOK * 64)
HI = lax.Precision.HIGHEST
NT = (((1,), (1,)), ((), ()))
TN = (((0,), (0,)), ((), ()))
NN = (((1,), (0,)), ((), ()))


def mm(a, b, dims):
    return lax.dot_general(a, b, dims, preferred_element_type=f32)


def permute(v, target):
    pairs = []
    for z in range(NZ):
        for y in range(NY):
            for c in range(2):
                for x in range(NX):
                    tz, ty, tc, tx = target(z, y, c, x)
                    src = ((z * NY + y) * 2 + c) * NX + x
                    dst = ((tz * NY + ty) * 2 + tc) * NX + tx
                    pairs.append((src, dst))
    return lax.ppermute(v, BOTH, pairs)


def swap_core(z, y, c, x):
    return z, y, 1 - c, x


def first_axis(k):
    return lambda z, y, c, x: (z, y, c, (x + k) % NX) if c == 0 else (z, (y + k) % NY, c, x)


def second_axis(k):
    return lambda z, y, c, x: (z, (y + k) % NY, c, x) if c == 0 else (z, y, c, (x + k) % NX)


def x_axis(k):
    return lambda z, y, c, x: (z, y, c, (x + k) % NX)


def rate_lanes(rate_ref, width):
    lane = lax.broadcasted_iota(jnp.int32, (1, width), 1) // (width // HEADS)
    rates = jnp.zeros((1, width), f32)
    for h in range(HEADS):
        rates = jnp.where(lane == h, rate_ref[h] * RATE_UNIT, rates)
    return rates


def signed_tri():
    t = lax.broadcasted_iota(jnp.int32, (TOK, TOK), 0)
    s = lax.broadcasted_iota(jnp.int32, (TOK, TOK), 1)
    half = TOK // 2
    plus = (s >= half) & (s <= t)
    minus = (s < half) & (s > t)
    return jnp.where(plus, 1.0, jnp.where(minus, -1.0, 0.0)).astype(f32)


def step_lanes(cum, dt_lanes):
    ones = jnp.ones((8, TOK // 2), f32)
    start = -lax.dot_general(ones, dt_lanes[:, : TOK // 2], NT, precision=HI, preferred_element_type=f32)[:1]
    row = lax.broadcasted_iota(jnp.int32, (TOK, CH), 0)
    return jnp.where(row == 0, cum - start, cum - pltpu.roll(cum, 1, 0)), start


def gate(v):
    s = 1.0 - v * (1.0 / 8.0)
    for n in (7.0, 6.0, 5.0, 4.0, 3.0, 2.0):
        s = 1.0 - v * (1.0 / n) * s
    return jnp.sqrt(jnp.where(v < 0.25, v * s, 1.0 - jnp.exp(-v)))


def local_forward(pos_ref, rate_ref, x_ref, b_ref, dt_ref, mine_ref, send_ref, tot_ref, xw_ref, xt_ref, cum_ref):
    dt = dt_ref[...].astype(f32)
    dt_lanes = jnp.broadcast_to(dt[:, None, :], (HEADS, HEAD_DIM, TOK)).reshape(CH, TOK)
    cum = lax.dot_general(signed_tri(), dt_lanes, NT, precision=HI, preferred_element_type=f32)
    cum_ref[...] = cum
    rate = rate_lanes(rate_ref, CH)
    xw = x_ref[...].astype(f32) * gate(step_lanes(cum, dt_lanes)[0] * (2.0 * rate))
    xw_ref[...] = xw.astype(bf16)
    xt = (xw * jnp.exp((cum - cum[TOK - 1:]) * rate)).astype(bf16)
    xt_ref[...] = xt
    own = mm(xt, b_ref[...], TN)
    head = lax.broadcasted_iota(jnp.int32, (HEADS, 1), 0)
    rate_col = jnp.zeros((HEADS, 1), f32)
    for h in range(HEADS):
        rate_col = jnp.where(head == h, rate_ref[h] * RATE_UNIT, rate_col)
    tot = jnp.broadcast_to(-(jnp.sum(dt, axis=1, keepdims=True) * rate_col), (HEADS, STATE))
    tot_ref[...] = tot
    send_ref[HALF:, :] = tot
    core = pos_ref[2]

    @pl.when(core == 0)
    def _():
        mine_ref[...] = own[:HALF]
        send_ref[:HALF, :] = own[HALF:]

    @pl.when(core == 1)
    def _():
        mine_ref[...] = own[HALF:]
        send_ref[:HALF, :] = own[:HALF]


def local_backward(pos_ref, rate_ref, cum_ref, dt_ref, c_ref, w_ref, g_ref, mine_ref, send_ref, gy_ref, gyd_ref, wide_ref):
    dt = dt_ref[...].astype(f32)
    dt_lanes = jnp.broadcast_to(dt[:, None, :], (HEADS, HEAD_DIM, TOK)).reshape(CH, TOK)
    rate = rate_lanes(rate_ref, CH)
    cum = cum_ref[...]
    start = step_lanes(cum, dt_lanes)[1]
    wide_ref[...] = g_ref[...].astype(f32)
    gy = mm(g_ref[...], w_ref[...], NT).astype(bf16)
    gy_ref[...] = gy
    gyd = (gy.astype(f32) * jnp.exp((start - cum) * rate)).astype(bf16)
    gyd_ref[...] = gyd
    adj = mm(gyd, c_ref[...], TN)
    core = pos_ref[2]

    @pl.when(core == 0)
    def _():
        mine_ref[...] = adj[:HALF]
        send_ref[...] = adj[HALF:]

    @pl.when(core == 1)
    def _():
        mine_ref[...] = adj[HALF:]
        send_ref[...] = adj[:HALF]


def my_heads(core, tots):
    return jnp.where(core == 0, tots[:HEADS // 2], tots[HEADS // 2:])


def decay_rows(tots):
    rows = jnp.exp(tots)
    return jnp.broadcast_to(rows[:, None, :], (HEADS // 2, HEAD_DIM, STATE)).reshape(HALF, STATE)


def chip_forward(pos_ref, mine_ref, peer_ref, tot_ref, out_ref):
    core = pos_ref[2]
    own = my_heads(core, tot_ref[...])
    other = my_heads(core, peer_ref[HALF:, :])
    mine, peer = mine_ref[...], peer_ref[:HALF, :]
    second = decay_rows(jnp.where(core == 0, other, own))
    chip = jnp.where(core == 0, mine, peer) * second + jnp.where(core == 0, peer, mine)
    out_ref[:, :PIECE, :] = chip.reshape(CHIPS, PIECE, STATE)
    tots = jnp.broadcast_to((own + other)[:, None, None, :], (HEADS // 2, CHIPS // (HEADS // 2), PIECE, STATE))
    out_ref[:, PIECE:, :] = tots.reshape(CHIPS, PIECE, STATE)


def scan_forward(pos_ref, in_ref, mine_ref, peer_ref, tot_ref, fpeer_ref, out_ref):
    core = pos_ref[2]
    first = decay_rows(my_heads(core, jnp.where(core == 0, tot_ref[...], fpeer_ref[HALF:, :])))
    mine, peer = mine_ref[...], peer_ref[...]
    chip = jnp.where(core == 0, mine, peer) + jnp.where(core == 0, peer, mine) * first
    out_ref[:, PIECE:, :] = chip.reshape(CHIPS, PIECE, STATE)
    acc = jnp.zeros((PIECE, STATE), f32)
    for k in range(CHIPS):
        out_ref[k, :PIECE, :] = acc
        acc = acc * jnp.exp(in_ref[k, PIECE:, :]) + in_ref[k, :PIECE, :]


def scan_backward(dec_ref, in_ref, out_ref):
    acc = jnp.zeros((PIECE, STATE), f32)
    for k in range(CHIPS - 1, -1, -1):
        out_ref[k] = acc
        acc = acc * jnp.exp(dec_ref[k, PIECE:, :]) + in_ref[k, PIECE:, :]


def core_forward(pos_ref, got_ref, mine_ref, peer_ref, tot_ref, keep_ref, send_ref):
    core = pos_ref[2]
    into = got_ref[:, :PIECE, :].reshape(HALF, STATE)
    first = decay_rows(my_heads(core, jnp.where(core == 0, tot_ref[...], peer_ref[HALF:, :])))
    after = into * first + jnp.where(core == 0, mine_ref[...], peer_ref[:HALF, :])
    keep_ref[...] = jnp.where(core == 0, into, after)
    send_ref[...] = jnp.where(core == 0, after, into)


def core_backward(pos_ref, got_ref, mine_ref, peer_ref, tot_ref, fpeer_ref, keep_ref, send_ref):
    core = pos_ref[2]
    after = got_ref[...].reshape(HALF, STATE)
    second = decay_rows(my_heads(core, jnp.where(core == 0, fpeer_ref[HALF:, :], tot_ref[...])))
    into = after * second + jnp.where(core == 0, peer_ref[...], mine_ref[...])
    keep_ref[...] = jnp.where(core == 0, into, after)
    send_ref[...] = jnp.where(core == 0, after, into)


def both_halves(core, keep, recv):
    low = jnp.where(core == 0, keep, recv)
    high = jnp.where(core == 0, recv, keep)
    return jnp.concatenate([low, high], axis=0).astype(bf16)


def intra(rate_ref, dt_ref, cum_ref, b_ref, c_ref, gy_ref, xw_ref,
          y_ref, gin_ref, wt_ref, hd_ref, gr_ref, gw_ref):
    dt = dt_ref[...].astype(f32)
    tri = signed_tri()
    cum_rows = lax.dot_general(dt, tri, NT, precision=HI, preferred_element_type=f32)
    rate = rate_lanes(rate_ref, CH)
    cum = cum_ref[...]
    i = lax.broadcasted_iota(jnp.int32, (TOK, TOK), 0)
    j = lax.broadcasted_iota(jnp.int32, (TOK, TOK), 1)
    lower = i >= j
    b = b_ref[...]
    c = c_ref[...]
    scores = mm(c, b, NT)
    pairs = jnp.zeros((TOK, TOK), f32)
    for h in range(HEADS):
        lanes = slice(h * HEAD_DIM, (h + 1) * HEAD_DIM)
        r = rate_ref[h] * RATE_UNIT
        gap = cum_rows[h:h + 1, :] - cum[:, h * HEAD_DIM:h * HEAD_DIM + 1]
        mask = jnp.exp(jnp.where(lower, gap * r, -jnp.inf))
        mixed = (mask * scores).astype(bf16)
        xw = xw_ref[:, lanes]
        gy = gy_ref[:, lanes]
        y_ref[:, lanes] = mm(mixed, xw, NN)
        gin_ref[:, lanes] = mm(mixed, gy, TN)
        pairs = pairs + mask * mm(gy, xw, NT)
    pairs = pairs.astype(bf16)
    gr_ref[...] = mm(pairs, b, NN)
    gw_ref[...] = mm(pairs, c, TN)
    dt_lanes = jnp.broadcast_to(dt[:, None, :], (HEADS, HEAD_DIM, TOK)).reshape(CH, TOK)
    steps, start = step_lanes(cum, dt_lanes)
    w = gate(steps * (2.0 * rate))
    gin_ref[...] = gin_ref[...] * w
    wt_ref[...] = w * jnp.exp((cum - cum[TOK - 1:]) * rate)
    hd_ref[...] = jnp.exp((start - cum) * rate)


def select_rows(core, y_at):
    row = lax.broadcasted_iota(jnp.int32, (CH // 2, CH), 0)
    lane = lax.broadcasted_iota(jnp.int32, (CH // 2, CH), 1)
    y = (y_at + row // 64) % NY
    z = (row // 8) % NZ
    return jnp.where(lane == ((z * NY + y) * 2 + core) * 8 + row % 8, 1.0, 0.0).astype(bf16)


def forward_out(pos_ref, carry_ref, recv_ref, c_ref, y_ref, hd_ref, out_ref, mine_ref, other_ref):
    y_at, core = pos_ref[1], pos_ref[2]
    state = both_halves(core, carry_ref[...], recv_ref[...])
    out = (y_ref[...] + hd_ref[...] * mm(c_ref[...], state, NT)).astype(bf16)
    out_ref[...] = out
    mine_ref[...] = mm(select_rows(core, y_at), out, NT).astype(bf16)
    other_ref[...] = mm(select_rows(1 - core, y_at), out, NT)


def partial_grad(pos_ref, mine_ref, peer_ref, g_ref, gp_ref, s0_ref, s1_ref, s2_ref, s3_ref):
    core, x_at = pos_ref[2], pos_ref[3]
    outs = (s0_ref, s1_ref, s2_ref, s3_ref)
    mine = mine_ref[...]
    peer = peer_ref[...].astype(bf16)
    for xr in range(NX):
        at = pl.multiple_of(((x_at + xr) % NX) * BLK, 128)
        tile = mm(mine, g_ref[:, pl.ds(at, BLK)], NN)
        tile = tile + mm(peer, gp_ref[:, pl.ds(at, BLK)].astype(bf16), NN)

        @pl.when(core == 0)
        def _():
            for yr in range(NY):
                outs[xr][yr] = tile[yr * 64:(yr + 1) * 64]

        @pl.when(core == 1)
        def _():
            for yr in range(NY):
                outs[yr][xr] = tile[yr * 64:(yr + 1) * 64]


def other_grads(pos_ref, carry_ref, recv_ref, after_ref, recv2_ref, b_ref, gin_ref, wt_ref, gyd_ref, xt_ref, gr_ref, gw_ref,
                gi_ref, gwr_ref, grd_ref):
    core = pos_ref[2]
    state = both_halves(core, carry_ref[...], recv_ref[...])
    adj = both_halves(core, after_ref[...], recv2_ref[...])
    gi_ref[...] = (gin_ref[...] + wt_ref[...] * mm(b_ref[...], adj, NT)).astype(bf16)
    grd_ref[...] = (gr_ref[...] + mm(gyd_ref[...], state, NN)).astype(bf16)
    gwr_ref[...] = (gw_ref[...] + mm(xt_ref[...], adj, NN)).astype(bf16)


def place(pos_ref, r0_ref, r1_ref, r2_ref, r3_ref, out_ref):
    x_at = pos_ref[3]
    for k, ref in enumerate((r0_ref, r1_ref, r2_ref, r3_ref)):
        at = pl.multiple_of(((x_at + NX - k) % NX) * BLK, 128)
        out_ref[:, pl.ds(at, BLK)] = ref[...]


def call(body, outs, scalars, *args, us=1):
    specs = [pl.BlockSpec(memory_space=pltpu.SMEM)] * scalars
    specs += [pl.BlockSpec(memory_space=pltpu.VMEM)] * (len(args) - scalars)
    shapes = [jax.ShapeDtypeStruct(s, d) for s, d in outs]
    moved = sum(a.size * a.dtype.itemsize for a in args) + sum(s.size * s.dtype.itemsize for s in shapes)
    got = pl.pallas_call(
        body,
        out_shape=shapes,
        in_specs=specs,
        out_specs=[pl.BlockSpec(memory_space=pltpu.VMEM)] * len(shapes),
        cost_estimate=pl.CostEstimate(flops=us * 1_000_000_000, bytes_accessed=moved, transcendentals=0),
        compiler_params=pltpu.CompilerParams(vmem_limit_bytes=48 << 20),
        name=body.__name__,
    )(*args)
    return got if len(got) > 1 else got[0]


def shards(inputs, write_vecs, read_vecs, dt_code, a_rate, w_out, grad_out):
    at = lax.axis_index("seq")
    pos = jnp.stack([at >> 3, (at >> 1) & 3, at & 1, lax.axis_index("dp")]).astype(jnp.int32)
    x, b, c, dt, g = inputs[0], write_vecs[0], read_vecs[0], dt_code[0], grad_out[0]
    chips = [[q * 2 + core for q in range(CHIPS)] for core in range(2)]
    depth = [[(z * NY + y) * 2 + core for z in range(NZ)] for y in range(NY) for core in range(2)]

    def over(v, groups):
        return lax.all_to_all(v, "seq", 0, 0, axis_index_groups=groups, tiled=True)

    half, wide = ((HALF, STATE), f32), ((TOK, CH), f32)
    tokens, narrow = ((TOK, CH), bf16), ((TOK, STATE), f32)
    mine, send, tot, xw, xt, cum = call(
        local_forward, [half, ((HALF + 8, STATE), f32), ((HEADS, STATE), f32), tokens, tokens, wide],
        2, pos, a_rate, x, b, dt, us=2)
    peer = permute(send, swap_core)
    chip = call(chip_forward, [((CHIPS, 2 * PIECE, STATE), f32)], 1, pos, mine, peer, tot)
    pieces = over(chip, chips)

    cum2, g2 = lax.optimization_barrier((cum, g, chip))[:2]
    bmine, bsend, gy, gyd, g_wide = call(local_backward, [half, half, tokens, tokens, ((TOK, D), f32)], 2, pos, a_rate, cum2, dt, c, w_out, g2, us=4)
    bpeer = permute(bsend, swap_core)
    y_in, gin, wt, hd, gr, gw = call(intra, [wide, wide, wide, wide, narrow, narrow], 1, a_rate, dt, cum2, b, c, gy, xw, us=3)
    pieces, bpeer, y_in, g_wide = lax.optimization_barrier((pieces, bpeer, y_in, g_wide))
    g_peer = permute(g_wide, swap_core)

    got = over(call(scan_forward, [((CHIPS, 2 * PIECE, STATE), f32)], 1, pos, pieces, bmine, bpeer, tot, peer), chips)
    carry, send = call(core_forward, [half, half], 1, pos, got, mine, peer, tot)
    recv = permute(send, swap_core)
    out, rows, send = call(
        forward_out, [tokens, ((CH // 2, TOK), bf16), ((CH // 2, TOK), f32)], 1, pos, carry, recv, c, y_in, hd, us=2)
    s = call(partial_grad, [((NY, 64, BLK), f32)] * 4, 1, pos, rows, permute(send, swap_core), g, g_peer, us=4)

    got2, pieces2 = lax.optimization_barrier((got, pieces, s[1]))[:2]
    back = over(call(scan_backward, [((CHIPS, PIECE, STATE), f32)], 0, pieces2, got2), chips)
    s1, s2, s3 = permute(s[1], first_axis(1)), permute(s[2], first_axis(2)), permute(s[3], first_axis(3))
    s1, s2, s3, back = lax.optimization_barrier((s1, s2, s3, back))
    s = s[0] + s2 + s1 + s3
    after, send = call(core_backward, [half, half], 1, pos, back, bmine, bpeer, tot, peer)
    recv2 = permute(send, swap_core)
    s = s[0] + permute(s[2], second_axis(2)) + permute(s[1], second_axis(1)) + permute(s[3], second_axis(3))
    s = jnp.sum(over(s.reshape(NZ, 8, BLK), depth), axis=0)
    grad_w_out = call(place, [((8, D), f32)], 1, pos, s, permute(s, x_axis(1)), permute(s, x_axis(2)),
                      permute(s, x_axis(3)))
    gi, gwr, grd = call(
        other_grads, [tokens, ((TOK, STATE), bf16), ((TOK, STATE), bf16)],
        1, pos, carry, recv, after, recv2, b, gin, wt, gyd, xt, gr, gw, us=2)
    return out[None], gi[None], gwr[None], grd[None], grad_w_out


def solution(mesh):
    rows = P("dp", "seq", None)
    return jax.shard_map(
        shards,
        mesh=mesh,
        in_specs=(rows, rows, rows, P("dp", None, "seq"), P(), P(), rows),
        out_specs=(rows, rows, rows, rows, P("seq", None)),
        check_vma=False,
    )
```

```python
import jax
import jax.numpy as jnp
from jax import lax
from jax.experimental import pallas as pl
from jax.experimental.pallas import tpu as pltpu
from jax.sharding import PartitionSpec as P

HEAD_DIM = 64
STATE = 128
HEADS = 8
TOK = 256
CH = HEADS * HEAD_DIM
D = 2560
NX, NY, NZ = 4, 4, 8
CHIPS = NY * NZ
HALF = CH // 2
PIECE = HALF // CHIPS
BLK = D // NX
BOTH = ("seq", "dp")

f32, bf16 = jnp.float32, jnp.bfloat16
RATE_UNIT = 1.0 / (8.0 * TOK * 64)
HI = lax.Precision.HIGHEST
NT = (((1,), (1,)), ((), ()))
TN = (((0,), (0,)), ((), ()))
NN = (((1,), (0,)), ((), ()))


def mm(a, b, dims):
    return lax.dot_general(a, b, dims, preferred_element_type=f32)


def permute(v, target):
    pairs = []
    for z in range(NZ):
        for y in range(NY):
            for c in range(2):
                for x in range(NX):
                    tz, ty, tc, tx = target(z, y, c, x)
                    src = ((z * NY + y) * 2 + c) * NX + x
                    dst = ((tz * NY + ty) * 2 + tc) * NX + tx
                    pairs.append((src, dst))
    return lax.ppermute(v, BOTH, pairs)


def swap_core(z, y, c, x):
    return z, y, 1 - c, x


def first_axis(k):
    return lambda z, y, c, x: (z, y, c, (x + k) % NX) if c == 0 else (z, (y + k) % NY, c, x)


def second_axis(k):
    return lambda z, y, c, x: (z, (y + k) % NY, c, x) if c == 0 else (z, y, c, (x + k) % NX)


def x_axis(k):
    return lambda z, y, c, x: (z, y, c, (x + k) % NX)


def place_of():
    at = lax.axis_index("seq")
    return at >> 3, (at >> 1) & 3, at & 1, lax.axis_index("dp")


def rate_lanes(rate_ref, width):
    lane = lax.broadcasted_iota(jnp.int32, (1, width), 1) // (width // HEADS)
    rates = jnp.zeros((1, width), f32)
    for h in range(HEADS):
        rates = jnp.where(lane == h, rate_ref[h] * RATE_UNIT, rates)
    return rates


def signed_tri():
    t = lax.broadcasted_iota(jnp.int32, (TOK, TOK), 0)
    s = lax.broadcasted_iota(jnp.int32, (TOK, TOK), 1)
    half = TOK // 2
    plus = (s >= half) & (s <= t)
    minus = (s < half) & (s > t)
    return jnp.where(plus, 1.0, jnp.where(minus, -1.0, 0.0)).astype(f32)


def step_lanes(cum, dt_lanes):
    ones = jnp.ones((8, TOK // 2), f32)
    start = -lax.dot_general(ones, dt_lanes[:, : TOK // 2], NT, precision=HI, preferred_element_type=f32)[:1]
    row = lax.broadcasted_iota(jnp.int32, (TOK, CH), 0)
    return jnp.where(row == 0, cum - start, cum - pltpu.roll(cum, 1, 0)), start


def gate(v):
    s = 1.0 - v * (1.0 / 8.0)
    for n in (7.0, 6.0, 5.0, 4.0, 3.0, 2.0):
        s = 1.0 - v * (1.0 / n) * s
    return jnp.sqrt(jnp.where(v < 0.25, v * s, 1.0 - jnp.exp(-v)))


def lanes_of(dt):
    return jnp.broadcast_to(dt[:, None, :], (HEADS, HEAD_DIM, TOK)).reshape(CH, TOK)


def local_forward(rate_ref, dt_ref, x_ref, b_ref, mine_ref, send_ref, tot_ref):
    core = place_of()[2]
    dt = dt_ref[...].astype(f32)
    rate = rate_lanes(rate_ref, CH)
    dt_lanes = lanes_of(dt)
    cum = lax.dot_general(signed_tri(), dt_lanes, NT, precision=HI, preferred_element_type=f32)
    w = gate(step_lanes(cum, dt_lanes)[0] * (2.0 * rate))
    xt = (x_ref[...].astype(f32) * w * jnp.exp((cum - cum[TOK - 1:]) * rate)).astype(bf16)
    own = mm(xt, b_ref[...], TN)
    head = lax.broadcasted_iota(jnp.int32, (HEADS, 1), 0)
    rate_col = jnp.zeros((HEADS, 1), f32)
    for h in range(HEADS):
        rate_col = jnp.where(head == h, rate_ref[h] * RATE_UNIT, rate_col)
    tot = jnp.broadcast_to(-(jnp.sum(dt, axis=1, keepdims=True) * rate_col), (HEADS, STATE))
    tot_ref[...] = tot
    send_ref[HALF:, :] = tot

    @pl.when(core == 0)
    def _():
        mine_ref[...] = own[:HALF]
        send_ref[:HALF, :] = own[HALF:]

    @pl.when(core == 1)
    def _():
        mine_ref[...] = own[HALF:]
        send_ref[:HALF, :] = own[:HALF]


def local_backward(rate_ref, dt_ref, c_ref, g_ref, w_ref, mine_ref, send_ref, gy_ref, wide_ref):
    core = place_of()[2]
    rate = rate_lanes(rate_ref, CH)
    dt_lanes = lanes_of(dt_ref[...].astype(f32))
    cum = lax.dot_general(signed_tri(), dt_lanes, NT, precision=HI, preferred_element_type=f32)
    decay = jnp.exp((step_lanes(cum, dt_lanes)[1] - cum) * rate)
    g = g_ref[...]
    gy = mm(g, w_ref[...], NT).astype(bf16)
    gy_ref[...] = gy
    wide_ref[...] = g.astype(f32)
    adj = mm((gy.astype(f32) * decay).astype(bf16), c_ref[...], TN)

    @pl.when(core == 0)
    def _():
        mine_ref[...] = adj[:HALF]
        send_ref[...] = adj[HALF:]

    @pl.when(core == 1)
    def _():
        mine_ref[...] = adj[HALF:]
        send_ref[...] = adj[:HALF]


def my_heads(core, tots):
    return jnp.where(core == 0, tots[:HEADS // 2], tots[HEADS // 2:])


def decay_rows(tots):
    rows = jnp.exp(tots)
    return jnp.broadcast_to(rows[:, None, :], (HEADS // 2, HEAD_DIM, STATE)).reshape(HALF, STATE)


def chip_forward(mine_ref, peer_ref, tot_ref, out_ref):
    core = place_of()[2]
    own = my_heads(core, tot_ref[...])
    other = my_heads(core, peer_ref[HALF:, :])
    mine, peer = mine_ref[...], peer_ref[:HALF, :]
    second = decay_rows(jnp.where(core == 0, other, own))
    chip = jnp.where(core == 0, mine, peer) * second + jnp.where(core == 0, peer, mine)
    out_ref[:, :PIECE, :] = chip.reshape(CHIPS, PIECE, STATE)
    tots = jnp.broadcast_to((own + other)[:, None, None, :], (HEADS // 2, CHIPS // (HEADS // 2), PIECE, STATE))
    out_ref[:, PIECE:, :] = tots.reshape(CHIPS, PIECE, STATE)


def scan_forward(in_ref, mine_ref, peer_ref, tot_ref, fpeer_ref, out_ref):
    core = place_of()[2]
    first = decay_rows(my_heads(core, jnp.where(core == 0, tot_ref[...], fpeer_ref[HALF:, :])))
    mine, peer = mine_ref[...], peer_ref[...]
    chip = jnp.where(core == 0, mine, peer) + jnp.where(core == 0, peer, mine) * first
    out_ref[:, PIECE:, :] = chip.reshape(CHIPS, PIECE, STATE)
    acc = jnp.zeros((PIECE, STATE), f32)
    for k in range(CHIPS):
        out_ref[k, :PIECE, :] = acc
        acc = acc * jnp.exp(in_ref[k, PIECE:, :]) + in_ref[k, :PIECE, :]


def scan_backward(dec_ref, in_ref, out_ref):
    acc = jnp.zeros((PIECE, STATE), f32)
    for k in range(CHIPS - 1, -1, -1):
        out_ref[k] = acc
        acc = acc * jnp.exp(dec_ref[k, PIECE:, :]) + in_ref[k, PIECE:, :]


def core_forward(got_ref, mine_ref, peer_ref, tot_ref, keep_ref, send_ref):
    core = place_of()[2]
    into = got_ref[:, :PIECE, :].reshape(HALF, STATE)
    first = decay_rows(my_heads(core, jnp.where(core == 0, tot_ref[...], peer_ref[HALF:, :])))
    after = into * first + jnp.where(core == 0, mine_ref[...], peer_ref[:HALF, :])
    keep_ref[...] = jnp.where(core == 0, into, after)
    send_ref[...] = jnp.where(core == 0, after, into)


def core_backward(got_ref, mine_ref, peer_ref, tot_ref, fpeer_ref, keep_ref, send_ref):
    core = place_of()[2]
    after = got_ref[...].reshape(HALF, STATE)
    second = decay_rows(my_heads(core, jnp.where(core == 0, fpeer_ref[HALF:, :], tot_ref[...])))
    into = after * second + jnp.where(core == 0, peer_ref[...], mine_ref[...])
    keep_ref[...] = jnp.where(core == 0, into, after)
    send_ref[...] = jnp.where(core == 0, after, into)


def both_halves(core, keep, recv):
    low = jnp.where(core == 0, keep, recv)
    high = jnp.where(core == 0, recv, keep)
    return jnp.concatenate([low, high], axis=0).astype(bf16)


def head_masks(rate_ref, dt, cum):
    cum_rows = lax.dot_general(dt, signed_tri(), NT, precision=HI, preferred_element_type=f32)
    i = lax.broadcasted_iota(jnp.int32, (TOK, TOK), 0)
    j = lax.broadcasted_iota(jnp.int32, (TOK, TOK), 1)
    for h in range(HEADS):
        gap = cum_rows[h:h + 1, :] - cum[:, h * HEAD_DIM:h * HEAD_DIM + 1]
        mask = jnp.exp(jnp.where(i >= j, gap * (rate_ref[h] * RATE_UNIT), -jnp.inf))
        yield slice(h * HEAD_DIM, (h + 1) * HEAD_DIM), mask


def intra_forward(rate_ref, dt_ref, x_ref, b_ref, c_ref, out_ref):
    dt = dt_ref[...].astype(f32)
    rate = rate_lanes(rate_ref, CH)
    dt_lanes = lanes_of(dt)
    cum = lax.dot_general(signed_tri(), dt_lanes, NT, precision=HI, preferred_element_type=f32)
    steps, start = step_lanes(cum, dt_lanes)
    xw = (x_ref[...].astype(f32) * gate(steps * (2.0 * rate))).astype(bf16)
    scores = mm(c_ref[...], b_ref[...], NT)
    for lanes, mask in head_masks(rate_ref, dt, cum):
        out_ref[:, lanes] = mm((mask * scores).astype(bf16), xw[:, lanes], NN)
    out_ref[:, CH:] = jnp.exp((start - cum) * rate)


def select_rows(core, y_at):
    row = lax.broadcasted_iota(jnp.int32, (CH // 2, CH), 0)
    lane = lax.broadcasted_iota(jnp.int32, (CH // 2, CH), 1)
    y = (y_at + row // 64) % NY
    z = (row // 8) % NZ
    return jnp.where(lane == ((z * NY + y) * 2 + core) * 8 + row % 8, 1.0, 0.0).astype(bf16)


def forward_out(keep_ref, recv_ref, c_ref, y_ref, out_ref, mine_ref, other_ref):
    _, y_at, core, _ = place_of()
    state = both_halves(core, keep_ref[...], recv_ref[...])
    out = (y_ref[:, :CH] + y_ref[:, CH:] * mm(c_ref[...], state, NT)).astype(bf16)
    out_ref[...] = out
    mine_ref[...] = mm(select_rows(core, y_at), out, NT).astype(bf16)
    other_ref[...] = mm(select_rows(1 - core, y_at), out, NT)


def partial_grad(rows_ref, peer_ref, g_ref, gp_ref, s0_ref, s1_ref, s2_ref, s3_ref):
    _, _, core, x_at = place_of()
    outs = (s0_ref, s1_ref, s2_ref, s3_ref)
    mine = rows_ref[...]
    peer = peer_ref[...].astype(bf16)
    for xr in range(NX):
        at = pl.multiple_of(((x_at + xr) % NX) * BLK, 128)
        tile = mm(mine, g_ref[:, pl.ds(at, BLK)], NN)
        tile = tile + mm(peer, gp_ref[:, pl.ds(at, BLK)].astype(bf16), NN)

        @pl.when(core == 0)
        def _():
            for yr in range(NY):
                outs[xr][yr] = tile[yr * 64:(yr + 1) * 64]

        @pl.when(core == 1)
        def _():
            for yr in range(NY):
                outs[yr][xr] = tile[yr * 64:(yr + 1) * 64]


def gradients(rate_ref, dt_ref, x_ref, b_ref, c_ref, gy_ref, keep_ref, recv_ref, after_ref, recv2_ref,
              gi_ref, gwr_ref, grd_ref):
    core = place_of()[2]
    dt = dt_ref[...].astype(f32)
    rate = rate_lanes(rate_ref, CH)
    dt_lanes = lanes_of(dt)
    cum = lax.dot_general(signed_tri(), dt_lanes, NT, precision=HI, preferred_element_type=f32)
    steps, start = step_lanes(cum, dt_lanes)
    w = gate(steps * (2.0 * rate))
    tail = jnp.exp((cum - cum[TOK - 1:]) * rate)
    xw = x_ref[...].astype(f32) * w
    xt = (xw * tail).astype(bf16)
    xw = xw.astype(bf16)
    gy = gy_ref[...]
    gyd = (gy.astype(f32) * jnp.exp((start - cum) * rate)).astype(bf16)
    b = b_ref[...]
    c = c_ref[...]
    scores = mm(c, b, NT)
    state = both_halves(core, keep_ref[...], recv_ref[...])
    adj = both_halves(core, after_ref[...], recv2_ref[...])
    inter = tail * mm(b, adj, NT)
    pairs = jnp.zeros((TOK, TOK), f32)
    for lanes, mask in head_masks(rate_ref, dt, cum):
        intra = mm((mask * scores).astype(bf16), gy[:, lanes], TN)
        gi_ref[:, lanes] = (w[:, lanes] * (intra + inter[:, lanes])).astype(bf16)
        pairs = pairs + mask * mm(gy[:, lanes], xw[:, lanes], NT)
    pairs = pairs.astype(bf16)
    grd_ref[...] = (mm(pairs, b, NN) + mm(gyd, state, NN)).astype(bf16)
    gwr_ref[...] = (mm(pairs, c, TN) + mm(xt, adj, NN)).astype(bf16)


def place(r0_ref, r1_ref, r2_ref, r3_ref, out_ref):
    x_at = place_of()[3]
    for k, ref in enumerate((r0_ref, r1_ref, r2_ref, r3_ref)):
        at = pl.multiple_of(((x_at + NX - k) % NX) * BLK, 128)
        out_ref[:, pl.ds(at, BLK)] = ref[...]


class Fetched:
    def __init__(self, copy, buffer):
        self.copy, self.buffer, self.here = copy, buffer, False

    def wait(self):
        if not self.here:
            self.copy.wait()
            self.here = True

    def __getitem__(self, at):
        self.wait()
        return self.buffer[at]


def call(body, outs, fetch, *args, us=1):
    shapes = [jax.ShapeDtypeStruct(s, d) for s, d in outs]
    moved = sum(a.size * a.dtype.itemsize for a in args) + sum(s.size * s.dtype.itemsize for s in shapes)
    scratch = [(pltpu.SMEM if a.ndim == 1 else pltpu.VMEM)(a.shape, a.dtype) for a in args[:fetch]]
    if fetch:
        scratch.append(pltpu.SemaphoreType.DMA((fetch,)))

    def kernel(*refs):
        left = refs[len(args) + len(outs):]
        held = [Fetched(pltpu.make_async_copy(refs[n], left[n], left[fetch].at[n]), left[n]) for n in range(fetch)]
        for one in held:
            one.copy.start()
        body(*held, *refs[fetch:len(args) + len(outs)])
        for one in held:
            one.wait()

    got = pl.pallas_call(
        kernel,
        out_shape=shapes,
        in_specs=[pl.BlockSpec(memory_space=pltpu.HBM)] * fetch
        + [pl.BlockSpec(memory_space=pltpu.VMEM)] * (len(args) - fetch),
        out_specs=[pl.BlockSpec(memory_space=pltpu.VMEM)] * len(shapes),
        scratch_shapes=scratch,
        cost_estimate=pl.CostEstimate(flops=us * 1_000_000_000, bytes_accessed=moved, transcendentals=0),
        compiler_params=pltpu.CompilerParams(vmem_limit_bytes=(54 << 20) if fetch else (8 << 20)),
        name=body.__name__,
    )(*args)
    return got if len(got) > 1 else got[0]


def shards(inputs, write_vecs, read_vecs, dt_code, a_rate, w_out, grad_out):
    x, b, c, dt, g = inputs[0], write_vecs[0], read_vecs[0], dt_code[0], grad_out[0]
    chips = [[q * 2 + core for q in range(CHIPS)] for core in range(2)]
    depth = [[(z * NY + y) * 2 + core for z in range(NZ)] for y in range(NY) for core in range(2)]

    def over(v, groups):
        return lax.all_to_all(v, "seq", 0, 0, axis_index_groups=groups, tiled=True)

    half = ((HALF, STATE), f32)
    tokens, narrow = ((TOK, CH), bf16), ((TOK, STATE), bf16)
    mine, send, tot = call(local_forward, [half, ((HALF + 8, STATE), f32), ((HEADS, STATE), f32)], 4,
                           a_rate, dt, x, b, us=2)
    peer = permute(send, swap_core)
    chip = call(chip_forward, [((CHIPS, 2 * PIECE, STATE), f32)], 0, mine, peer, tot)
    pieces = over(chip, chips)

    g2, x2 = lax.optimization_barrier((g, x, chip))[:2]
    bmine, bsend, gy, g_wide = call(local_backward, [half, half, tokens, ((TOK, D), f32)], 5,
                                    a_rate, dt, c, g2, w_out, us=4)
    bpeer = permute(bsend, swap_core)
    y_in = call(intra_forward, [((TOK, 2 * CH), f32)], 5, a_rate, dt, x2, b, c, us=3)
    pieces, bpeer, y_in, g_wide = lax.optimization_barrier((pieces, bpeer, y_in, g_wide))
    g_peer = permute(g_wide, swap_core)

    got = over(call(scan_forward, [((CHIPS, 2 * PIECE, STATE), f32)], 0, pieces, bmine, bpeer, tot, peer), chips)
    keep, send = call(core_forward, [half, half], 0, got, mine, peer, tot)
    recv = permute(send, swap_core)
    out, rows, send = call(
        forward_out, [tokens, ((HALF, TOK), bf16), ((HALF, TOK), f32)], 0, keep, recv, c, y_in, us=2)
    s = call(partial_grad, [((NY, 64, BLK), f32)] * 4, 0, rows, permute(send, swap_core), g, g_peer, us=4)

    got2, pieces2 = lax.optimization_barrier((got, pieces, s[1]))[:2]
    back = over(call(scan_backward, [((CHIPS, PIECE, STATE), f32)], 0, pieces2, got2), chips)
    s1, s2, s3 = permute(s[1], first_axis(1)), permute(s[2], first_axis(2)), permute(s[3], first_axis(3))
    s1, s2, s3, back = lax.optimization_barrier((s1, s2, s3, back))
    s = s[0] + s2 + s1 + s3
    after, send = call(core_backward, [half, half], 0, back, bmine, bpeer, tot, peer)
    recv2 = permute(send, swap_core)
    s = s[0] + permute(s[2], second_axis(2)) + permute(s[1], second_axis(1)) + permute(s[3], second_axis(3))
    s = over(s.reshape(NZ, 8, BLK), depth)
    gi, gwr, grd = call(gradients, [tokens, narrow, narrow], 5, a_rate, dt, x2, b, c, gy, keep, recv, after, recv2, us=5)
    s, gi = lax.optimization_barrier((s, gi))
    s = jnp.sum(s, axis=0)
    grad_w_out = call(place, [((8, D), f32)], 0, s, permute(s, x_axis(1)), permute(s, x_axis(2)), permute(s, x_axis(3)))
    return out[None], gi[None], gwr[None], grd[None], grad_w_out


def solution(mesh):
    rows = P("dp", "seq", None)
    return jax.shard_map(
        shards,
        mesh=mesh,
        in_specs=(rows, rows, rows, P("dp", None, "seq"), P(), P(), rows),
        out_specs=(rows, rows, rows, rows, P("seq", None)),
        check_vma=False,
    )
```

```python
import jax
import jax.numpy as jnp
from jax import lax
from jax.experimental import pallas as pl
from jax.experimental.pallas import tpu as pltpu
from jax.sharding import PartitionSpec as P

HEAD_DIM = 64
STATE = 128
HEADS = 8
TOK = 256
CH = HEADS * HEAD_DIM
D = 2560
NX, NY, NZ = 4, 4, 8
CHIPS = NY * NZ
HALF = CH // 2
PIECE = HALF // CHIPS
BLK = D // NX
BOTH = ("seq", "dp")

f32, bf16 = jnp.float32, jnp.bfloat16
RATE_UNIT = 1.0 / (8.0 * TOK * 64)
HI = lax.Precision.HIGHEST
NT = (((1,), (1,)), ((), ()))
TN = (((0,), (0,)), ((), ()))
NN = (((1,), (0,)), ((), ()))


def mm(a, b, dims):
    return lax.dot_general(a, b, dims, preferred_element_type=f32)


def permute(v, target):
    pairs = []
    for z in range(NZ):
        for y in range(NY):
            for c in range(2):
                for x in range(NX):
                    tz, ty, tc, tx = target(z, y, c, x)
                    src = ((z * NY + y) * 2 + c) * NX + x
                    dst = ((tz * NY + ty) * 2 + tc) * NX + tx
                    pairs.append((src, dst))
    return lax.ppermute(v, BOTH, pairs)


def swap_core(z, y, c, x):
    return z, y, 1 - c, x


def first_axis(k):
    return lambda z, y, c, x: (z, y, c, (x + k) % NX) if c == 0 else (z, (y + k) % NY, c, x)


def second_axis(k):
    return lambda z, y, c, x: (z, (y + k) % NY, c, x) if c == 0 else (z, y, c, (x + k) % NX)


def x_axis(k):
    return lambda z, y, c, x: (z, y, c, (x + k) % NX)


def place_of():
    at = lax.axis_index("seq")
    return at >> 3, (at >> 1) & 3, at & 1, lax.axis_index("dp")


def rate_rows(rate_ref):
    head = lax.broadcasted_iota(jnp.int32, (HEADS, 1), 0)
    rates = jnp.zeros((HEADS, 1), f32)
    for h in range(HEADS):
        rates = jnp.where(head == h, rate_ref[h] * RATE_UNIT, rates)
    return rates


def signed_tri():
    t = lax.broadcasted_iota(jnp.int32, (TOK, TOK), 0)
    s = lax.broadcasted_iota(jnp.int32, (TOK, TOK), 1)
    half = TOK // 2
    plus = (s >= half) & (s <= t)
    minus = (s < half) & (s > t)
    return jnp.where(plus, 1.0, jnp.where(minus, -1.0, 0.0)).astype(f32)


def row_sums(dt):
    return lax.dot_general(dt, signed_tri(), NT, precision=HI, preferred_element_type=f32)


def column_sums(dt):
    return lax.dot_general(signed_tri(), dt, NT, precision=HI, preferred_element_type=f32)


def before_first(dt):
    return -jnp.sum(dt[:, : TOK // 2], axis=1, keepdims=True)


def spread(rows):
    head = lax.broadcasted_iota(jnp.int32, (HEADS, CH), 0)
    lane = lax.broadcasted_iota(jnp.int32, (HEADS, CH), 1) // HEAD_DIM
    pick = jnp.where(head == lane, 1.0, 0.0).astype(f32)
    return lax.dot_general(rows, pick, TN, precision=HI, preferred_element_type=f32)


def gate(v):
    s = 1.0 - v * (1.0 / 8.0)
    for n in (7.0, 6.0, 5.0, 4.0, 3.0, 2.0):
        s = 1.0 - v * (1.0 / n) * s
    return jnp.sqrt(jnp.where(v < 0.25, v * s, 1.0 - jnp.exp(-v)))


def local_forward(rate_ref, dt_ref, x_ref, b_ref, mine_ref, send_ref):
    core = place_of()[2]
    dt = dt_ref[...].astype(f32)
    rate = rate_rows(rate_ref)
    cum = row_sums(dt)
    tail = jnp.exp((cum - cum[:, TOK - 1:]) * rate)
    xt = (x_ref[...].astype(f32) * spread(gate(dt * (2.0 * rate)) * tail)).astype(bf16)
    own = mm(xt, b_ref[...], TN)
    tot = jnp.broadcast_to(-(jnp.sum(dt, axis=1, keepdims=True) * rate), (HEADS, STATE))
    mine_ref[HALF:, :] = tot
    send_ref[HALF:, :] = tot

    @pl.when(core == 0)
    def _():
        mine_ref[:HALF, :] = own[:HALF]
        send_ref[:HALF, :] = own[HALF:]

    @pl.when(core == 1)
    def _():
        mine_ref[:HALF, :] = own[HALF:]
        send_ref[:HALF, :] = own[:HALF]


def local_backward(rate_ref, dt_ref, c_ref, g_ref, w_ref, mine_ref, send_ref, gy_ref, wide_ref):
    core = place_of()[2]
    dt = dt_ref[...].astype(f32)
    decay = spread(jnp.exp((before_first(dt) - row_sums(dt)) * rate_rows(rate_ref)))
    g = g_ref[...]
    wide_ref[...] = g.astype(f32)
    gy = mm(g, w_ref[...], NT).astype(bf16)
    gy_ref[...] = gy
    adj = mm((gy.astype(f32) * decay).astype(bf16), c_ref[...], TN)

    @pl.when(core == 0)
    def _():
        mine_ref[...] = adj[:HALF]
        send_ref[...] = adj[HALF:]

    @pl.when(core == 1)
    def _():
        mine_ref[...] = adj[HALF:]
        send_ref[...] = adj[:HALF]


def my_heads(core, tots):
    return jnp.where(core == 0, tots[:HEADS // 2], tots[HEADS // 2:])


def decay_rows(tots):
    rows = jnp.exp(tots)
    return jnp.broadcast_to(rows[:, None, :], (HEADS // 2, HEAD_DIM, STATE)).reshape(HALF, STATE)


def chip_forward(mine_ref, peer_ref, out_ref):
    core = place_of()[2]
    own = my_heads(core, mine_ref[HALF:, :])
    other = my_heads(core, peer_ref[HALF:, :])
    mine, peer = mine_ref[:HALF, :], peer_ref[:HALF, :]
    second = decay_rows(jnp.where(core == 0, other, own))
    chip = jnp.where(core == 0, mine, peer) * second + jnp.where(core == 0, peer, mine)
    rows = chip.reshape(CHIPS, PIECE, STATE)
    for r in range(PIECE):
        out_ref[:, 0, r * STATE:(r + 1) * STATE] = rows[:, r, :]
    tots = jnp.broadcast_to((own + other)[:, None, :], (HEADS // 2, CHIPS // (HEADS // 2), STATE))
    out_ref[:, 0, PIECE * STATE:] = tots.reshape(CHIPS, STATE)


def scan_forward(in_ref, mine_ref, peer_ref, fmine_ref, fpeer_ref, out_ref):
    core = place_of()[2]
    first = decay_rows(my_heads(core, jnp.where(core == 0, fmine_ref[HALF:, :], fpeer_ref[HALF:, :])))
    mine, peer = mine_ref[...], peer_ref[...]
    chip = jnp.where(core == 0, mine, peer) + jnp.where(core == 0, peer, mine) * first
    out_ref[:, PIECE:, :] = chip.reshape(CHIPS, PIECE, STATE)
    acc = [jnp.zeros((1, STATE), f32)] * PIECE
    for k in range(CHIPS):
        keep = jnp.exp(in_ref[k, :, PIECE * STATE:])
        for r in range(PIECE):
            out_ref[k, r:r + 1, :] = acc[r]
            acc[r] = acc[r] * keep + in_ref[k, :, r * STATE:(r + 1) * STATE]


def scan_backward(dec_ref, in_ref, out_ref):
    acc = jnp.zeros((PIECE, STATE), f32)
    for k in range(CHIPS - 1, -1, -1):
        out_ref[k] = acc
        acc = acc * jnp.exp(dec_ref[k, :, PIECE * STATE:]) + in_ref[k, PIECE:, :]


def core_forward(got_ref, mine_ref, peer_ref, keep_ref, send_ref):
    core = place_of()[2]
    into = got_ref[:, :PIECE, :].reshape(HALF, STATE)
    first = decay_rows(my_heads(core, jnp.where(core == 0, mine_ref[HALF:, :], peer_ref[HALF:, :])))
    after = into * first + jnp.where(core == 0, mine_ref[:HALF, :], peer_ref[:HALF, :])
    keep_ref[...] = jnp.where(core == 0, into, after)
    send_ref[...] = jnp.where(core == 0, after, into)


def core_backward(got_ref, mine_ref, peer_ref, fmine_ref, fpeer_ref, keep_ref, send_ref):
    core = place_of()[2]
    after = got_ref[...].reshape(HALF, STATE)
    second = decay_rows(my_heads(core, jnp.where(core == 0, fpeer_ref[HALF:, :], fmine_ref[HALF:, :])))
    into = after * second + jnp.where(core == 0, peer_ref[...], mine_ref[...])
    keep_ref[...] = jnp.where(core == 0, into, after)
    send_ref[...] = jnp.where(core == 0, after, into)


def both_halves(core, keep, recv):
    low = jnp.where(core == 0, keep, recv)
    high = jnp.where(core == 0, recv, keep)
    return jnp.concatenate([low, high], axis=0).astype(bf16)


def intra_forward(rate_ref, dt_ref, x_ref, b_ref, c_ref, out_ref):
    dt = dt_ref[...].astype(f32)
    rate = rate_rows(rate_ref)
    rows, cols = row_sums(dt), column_sums(dt)
    xw = (x_ref[...].astype(f32) * spread(gate(dt * (2.0 * rate)))).astype(bf16)
    scores = mm(c_ref[...], b_ref[...], NT)
    i = lax.broadcasted_iota(jnp.int32, (TOK, TOK), 0)
    j = lax.broadcasted_iota(jnp.int32, (TOK, TOK), 1)
    for h in range(HEADS):
        lanes = slice(h * HEAD_DIM, (h + 1) * HEAD_DIM)
        gap = (rows[h:h + 1, :] - cols[:, h:h + 1]) * (rate_ref[h] * RATE_UNIT)
        mask = jnp.exp(jnp.where(i >= j, gap, -jnp.inf))
        out_ref[:, lanes] = mm((mask * scores).astype(bf16), xw[:, lanes], NN)
    out_ref[:, CH:] = spread(jnp.exp((before_first(dt) - rows) * rate))


def select_rows(core, y_at):
    row = lax.broadcasted_iota(jnp.int32, (CH // 2, CH), 0)
    lane = lax.broadcasted_iota(jnp.int32, (CH // 2, CH), 1)
    y = (y_at + row // 64) % NY
    z = (row // 8) % NZ
    return jnp.where(lane == ((z * NY + y) * 2 + core) * 8 + row % 8, 1.0, 0.0).astype(bf16)


def forward_out(keep_ref, recv_ref, c_ref, y_ref, out_ref, mine_ref, other_ref):
    _, y_at, core, _ = place_of()
    state = both_halves(core, keep_ref[...], recv_ref[...])
    out = (y_ref[:, :CH] + y_ref[:, CH:] * mm(c_ref[...], state, NT)).astype(bf16)
    out_ref[...] = out
    mine_ref[...] = mm(select_rows(core, y_at), out, NT).astype(bf16)
    other_ref[...] = mm(select_rows(1 - core, y_at), out, NT)


def partial_grad(rows_ref, peer_ref, g_ref, gp_ref, s0_ref, s1_ref, s2_ref, s3_ref):
    _, _, core, x_at = place_of()
    outs = (s0_ref, s1_ref, s2_ref, s3_ref)
    mine = rows_ref[...]
    peer = peer_ref[...].astype(bf16)
    for xr in range(NX):
        at = pl.multiple_of(((x_at + xr) % NX) * BLK, 128)
        tile = mm(mine, g_ref[:, pl.ds(at, BLK)], NN)
        tile = tile + mm(peer, gp_ref[:, pl.ds(at, BLK)].astype(bf16), NN)

        @pl.when(core == 0)
        def _():
            for yr in range(NY):
                outs[xr][yr] = tile[yr * 64:(yr + 1) * 64]

        @pl.when(core == 1)
        def _():
            for yr in range(NY):
                outs[yr][xr] = tile[yr * 64:(yr + 1) * 64]


def gradients(rate_ref, dt_ref, x_ref, b_ref, c_ref, gy_ref, keep_ref, recv_ref, after_ref, recv2_ref,
              gi_ref, gwr_ref, grd_ref):
    core = place_of()[2]
    dt = dt_ref[...].astype(f32)
    rate = rate_rows(rate_ref)
    rows, cols = row_sums(dt), column_sums(dt)
    gates = gate(dt * (2.0 * rate))
    w = spread(gates)
    wt = spread(gates * jnp.exp((rows - rows[:, TOK - 1:]) * rate))
    x = x_ref[...].astype(f32)
    xw, xt = (x * w).astype(bf16), (x * wt).astype(bf16)
    gy = gy_ref[...]
    gyd = (gy.astype(f32) * spread(jnp.exp((before_first(dt) - rows) * rate))).astype(bf16)
    b = b_ref[...]
    c = c_ref[...]
    scores = mm(b, c, NT)
    j = lax.broadcasted_iota(jnp.int32, (TOK, TOK), 0)
    i = lax.broadcasted_iota(jnp.int32, (TOK, TOK), 1)
    state = both_halves(core, keep_ref[...], recv_ref[...])
    adj = both_halves(core, after_ref[...], recv2_ref[...])
    inter = wt * mm(b, adj, NT)
    pairs = jnp.zeros((TOK, TOK), f32)
    for h in range(HEADS):
        lanes = slice(h * HEAD_DIM, (h + 1) * HEAD_DIM)
        gap = (cols[:, h:h + 1] - rows[h:h + 1, :]) * (rate_ref[h] * RATE_UNIT)
        mask = jnp.exp(jnp.where(i >= j, gap, -jnp.inf))
        intra = mm((mask * scores).astype(bf16), gy[:, lanes], NN)
        gi_ref[:, lanes] = (w[:, lanes] * intra + inter[:, lanes]).astype(bf16)
        pairs = pairs + mask * mm(xw[:, lanes], gy[:, lanes], NT)
    pairs = pairs.astype(bf16)
    grd_ref[...] = (mm(pairs, b, TN) + mm(gyd, state, NN)).astype(bf16)
    gwr_ref[...] = (mm(pairs, c, NN) + mm(xt, adj, NN)).astype(bf16)


def place(r0_ref, r1_ref, r2_ref, r3_ref, out_ref):
    x_at = place_of()[3]
    for k, ref in enumerate((r0_ref, r1_ref, r2_ref, r3_ref)):
        at = pl.multiple_of(((x_at + NX - k) % NX) * BLK, 128)
        out_ref[:, pl.ds(at, BLK)] = ref[...]


class Fetched:
    def __init__(self, copy, buffer):
        self.copy, self.buffer, self.here = copy, buffer, False

    def wait(self):
        if not self.here:
            self.copy.wait()
            self.here = True

    def __getitem__(self, at):
        self.wait()
        return self.buffer[at]


def call(body, outs, fetch, *args, us=1):
    shapes = [jax.ShapeDtypeStruct(s, d) for s, d in outs]
    moved = sum(a.size * a.dtype.itemsize for a in args) + sum(s.size * s.dtype.itemsize for s in shapes)
    scratch = [(pltpu.SMEM if a.ndim == 1 else pltpu.VMEM)(a.shape, a.dtype) for a in args[:fetch]]
    if fetch:
        scratch.append(pltpu.SemaphoreType.DMA((fetch,)))

    def kernel(*refs):
        left = refs[len(args) + len(outs):]
        held = [Fetched(pltpu.make_async_copy(refs[n], left[n], left[fetch].at[n]), left[n]) for n in range(fetch)]
        for one in held:
            one.copy.start()
        body(*held, *refs[fetch:len(args) + len(outs)])
        for one in held:
            one.wait()

    got = pl.pallas_call(
        kernel,
        out_shape=shapes,
        in_specs=[pl.BlockSpec(memory_space=pltpu.HBM)] * fetch
        + [pl.BlockSpec(memory_space=pltpu.VMEM)] * (len(args) - fetch),
        out_specs=[pl.BlockSpec(memory_space=pltpu.VMEM)] * len(shapes),
        scratch_shapes=scratch,
        cost_estimate=pl.CostEstimate(flops=us * 1_000_000_000, bytes_accessed=moved, transcendentals=0),
        compiler_params=pltpu.CompilerParams(vmem_limit_bytes=(54 << 20) if fetch else (8 << 20)),
        name=body.__name__,
    )(*args)
    return got if len(got) > 1 else got[0]


def shards(inputs, write_vecs, read_vecs, dt_code, a_rate, w_out, grad_out):
    x, b, c, dt, g = inputs[0], write_vecs[0], read_vecs[0], dt_code[0], grad_out[0]
    chips = [[q * 2 + core for q in range(CHIPS)] for core in range(2)]
    depth = [[(z * NY + y) * 2 + core for z in range(NZ)] for y in range(NY) for core in range(2)]

    def over(v, groups):
        return lax.all_to_all(v, "seq", 0, 0, axis_index_groups=groups, tiled=True)

    half = ((HALF, STATE), f32)
    tokens, narrow = ((TOK, CH), bf16), ((TOK, STATE), bf16)
    both = ((HALF + 8, STATE), f32)
    mine, send = call(local_forward, [both, both], 4, a_rate, dt, x, b, us=2)
    peer = permute(send, swap_core)
    chip = call(chip_forward, [((CHIPS, 1, (PIECE + 1) * STATE), f32)], 0, mine, peer)
    pieces = over(chip, chips)

    g2 = lax.optimization_barrier((g, chip))[0]
    bmine, bsend, gy, g_wide = call(local_backward, [half, half, tokens, ((TOK, D), f32)], 5,
                                    a_rate, dt, c, g2, w_out, us=4)
    bpeer = permute(bsend, swap_core)
    pieces, bpeer, g_wide = lax.optimization_barrier((pieces, bpeer, g_wide))
    g_peer = permute(g_wide, swap_core)
    back = call(scan_forward, [((CHIPS, 2 * PIECE, STATE), f32)], 0, pieces, bmine, bpeer, mine, peer)
    got = over(back, chips)
    x2 = lax.optimization_barrier((x, back))[0]
    y_in = call(intra_forward, [((TOK, 2 * CH), f32)], 5, a_rate, dt, x2, b, c, us=3)
    got, y_in = lax.optimization_barrier((got, y_in))
    keep, send = call(core_forward, [half, half], 0, got, mine, peer)
    recv = permute(send, swap_core)
    out, rows, send = call(
        forward_out, [tokens, ((HALF, TOK), bf16), ((HALF, TOK), f32)], 0, keep, recv, c, y_in, us=2)
    s = call(partial_grad, [((NY, 64, BLK), f32)] * 4, 0, rows, permute(send, swap_core), g, g_peer, us=4)

    got2, pieces2 = lax.optimization_barrier((got, pieces, s[1]))[:2]
    back = over(call(scan_backward, [((CHIPS, PIECE, STATE), f32)], 0, pieces2, got2), chips)
    s1, s2, s3 = permute(s[1], first_axis(1)), permute(s[2], first_axis(2)), permute(s[3], first_axis(3))
    s1, s2, s3, back = lax.optimization_barrier((s1, s2, s3, back))
    s = s[0] + s2 + s1 + s3
    after, send = call(core_backward, [half, half], 0, back, bmine, bpeer, mine, peer)
    recv2 = permute(send, swap_core)
    s = s[0] + permute(s[2], second_axis(2)) + permute(s[1], second_axis(1)) + permute(s[3], second_axis(3))
    s = over(s.reshape(NZ, 8, BLK), depth)
    gi, gwr, grd = call(gradients, [tokens, narrow, narrow], 10, a_rate, dt, x2, b, c, gy, keep, recv, after, recv2, us=5)
    s, gi = lax.optimization_barrier((s, gi))
    s = jnp.sum(s, axis=0)
    grad_w_out = call(place, [((8, D), f32)], 0, s, permute(s, x_axis(1)), permute(s, x_axis(2)), permute(s, x_axis(3)))
    return out[None], gi[None], gwr[None], grd[None], grad_w_out


def solution(mesh):
    rows = P("dp", "seq", None)
    return jax.shard_map(
        shards,
        mesh=mesh,
        in_specs=(rows, rows, rows, P("dp", None, "seq"), P(), P(), rows),
        out_specs=(rows, rows, rows, rows, P("seq", None)),
        check_vma=False,
    )
```

```python
import jax
import jax.numpy as jnp
from jax import lax
from jax.experimental import pallas as pl
from jax.experimental.pallas import tpu as pltpu
from jax.sharding import PartitionSpec as P

HEAD_DIM = 64
STATE = 128
HEADS = 8
TOK = 256
CH = HEADS * HEAD_DIM
D = 2560
NX, NY, NZ = 4, 4, 8
CHIPS = NY * NZ
HALF = CH // 2
PIECE = HALF // CHIPS
BLK = D // NX
BOTH = ("seq", "dp")

f32, bf16 = jnp.float32, jnp.bfloat16
RATE_UNIT = 1.0 / (8.0 * TOK * 64)
HI = lax.Precision.HIGHEST
NT = (((1,), (1,)), ((), ()))
TN = (((0,), (0,)), ((), ()))
NN = (((1,), (0,)), ((), ()))


def mm(a, b, dims):
    return lax.dot_general(a, b, dims, preferred_element_type=f32)


def permute(v, target):
    pairs = []
    for z in range(NZ):
        for y in range(NY):
            for c in range(2):
                for x in range(NX):
                    tz, ty, tc, tx = target(z, y, c, x)
                    src = ((z * NY + y) * 2 + c) * NX + x
                    dst = ((tz * NY + ty) * 2 + tc) * NX + tx
                    pairs.append((src, dst))
    return lax.ppermute(v, BOTH, pairs)


def swap_core(z, y, c, x):
    return z, y, 1 - c, x


def first_axis(k):
    return lambda z, y, c, x: (z, y, c, (x + k) % NX) if c == 0 else (z, (y + k) % NY, c, x)


def second_axis(k):
    return lambda z, y, c, x: (z, (y + k) % NY, c, x) if c == 0 else (z, y, c, (x + k) % NX)


def x_axis(k):
    return lambda z, y, c, x: (z, y, c, (x + k) % NX)


def place_of():
    at = lax.axis_index("seq")
    return at >> 3, (at >> 1) & 3, at & 1, lax.axis_index("dp")


def rate_rows(rate_ref):
    head = lax.broadcasted_iota(jnp.int32, (HEADS, 1), 0)
    rates = jnp.zeros((HEADS, 1), f32)
    for h in range(HEADS):
        rates = jnp.where(head == h, rate_ref[h] * RATE_UNIT, rates)
    return rates


def signed_tri():
    t = lax.broadcasted_iota(jnp.int32, (TOK, TOK), 0)
    s = lax.broadcasted_iota(jnp.int32, (TOK, TOK), 1)
    half = TOK // 2
    plus = (s >= half) & (s <= t)
    minus = (s < half) & (s > t)
    return jnp.where(plus, 1.0, jnp.where(minus, -1.0, 0.0)).astype(f32)


def row_sums(dt):
    return lax.dot_general(dt, signed_tri(), NT, precision=HI, preferred_element_type=f32)


def column_sums(dt):
    return lax.dot_general(signed_tri(), dt, NT, precision=HI, preferred_element_type=f32)


def before_first(dt):
    return -jnp.sum(dt[:, : TOK // 2], axis=1, keepdims=True)


def spread(rows):
    head = lax.broadcasted_iota(jnp.int32, (HEADS, CH), 0)
    lane = lax.broadcasted_iota(jnp.int32, (HEADS, CH), 1) // HEAD_DIM
    pick = jnp.where(head == lane, 1.0, 0.0).astype(f32)
    return lax.dot_general(rows, pick, TN, precision=HI, preferred_element_type=f32)


def gate(v):
    s = 1.0 - v * (1.0 / 8.0)
    for n in (7.0, 6.0, 5.0, 4.0, 3.0, 2.0):
        s = 1.0 - v * (1.0 / n) * s
    return jnp.sqrt(jnp.where(v < 0.25, v * s, 1.0 - jnp.exp(-v)))


def local_forward(rate_ref, dt_ref, x_ref, b_ref, mine_ref, send_ref):
    core = place_of()[2]
    dt = dt_ref[...].astype(f32)
    rate = rate_rows(rate_ref)
    cum = row_sums(dt)
    tail = jnp.exp((cum - cum[:, TOK - 1:]) * rate)
    xt = (x_ref[...].astype(f32) * spread(gate(dt * (2.0 * rate)) * tail)).astype(bf16)
    own = mm(xt, b_ref[...], TN)
    tot = jnp.broadcast_to(-(jnp.sum(dt, axis=1, keepdims=True) * rate), (HEADS, STATE))
    mine_ref[HALF:, :] = tot
    send_ref[HALF:, :] = tot

    @pl.when(core == 0)
    def _():
        mine_ref[:HALF, :] = own[:HALF]
        send_ref[:HALF, :] = own[HALF:]

    @pl.when(core == 1)
    def _():
        mine_ref[:HALF, :] = own[HALF:]
        send_ref[:HALF, :] = own[:HALF]


def local_backward(rate_ref, dt_ref, c_ref, g_ref, w_ref, mine_ref, send_ref, gy_ref, wide_ref):
    core = place_of()[2]
    dt = dt_ref[...].astype(f32)
    decay = spread(jnp.exp((before_first(dt) - row_sums(dt)) * rate_rows(rate_ref)))
    g = g_ref[...]
    wide_ref[...] = g.astype(f32)
    gy = mm(g, w_ref[...], NT).astype(bf16)
    gy_ref[...] = gy
    adj = mm((gy.astype(f32) * decay).astype(bf16), c_ref[...], TN)

    @pl.when(core == 0)
    def _():
        mine_ref[...] = adj[:HALF]
        send_ref[...] = adj[HALF:]

    @pl.when(core == 1)
    def _():
        mine_ref[...] = adj[HALF:]
        send_ref[...] = adj[:HALF]


def my_heads(core, tots):
    return jnp.where(core == 0, tots[:HEADS // 2], tots[HEADS // 2:])


def decay_rows(tots):
    rows = jnp.exp(tots)
    return jnp.broadcast_to(rows[:, None, :], (HEADS // 2, HEAD_DIM, STATE)).reshape(HALF, STATE)


def chip_forward(mine_ref, peer_ref, out_ref):
    core = place_of()[2]
    own = my_heads(core, mine_ref[HALF:, :])
    other = my_heads(core, peer_ref[HALF:, :])
    mine, peer = mine_ref[:HALF, :], peer_ref[:HALF, :]
    second = decay_rows(jnp.where(core == 0, other, own))
    chip = jnp.where(core == 0, mine, peer) * second + jnp.where(core == 0, peer, mine)
    rows = chip.reshape(CHIPS, PIECE, STATE)
    for r in range(PIECE):
        out_ref[:, 0, r * STATE:(r + 1) * STATE] = rows[:, r, :]
    tots = jnp.broadcast_to((own + other)[:, None, :], (HEADS // 2, CHIPS // (HEADS // 2), STATE))
    out_ref[:, 0, PIECE * STATE:] = tots.reshape(CHIPS, STATE)


def scan_forward(in_ref, mine_ref, peer_ref, fmine_ref, fpeer_ref, out_ref):
    core = place_of()[2]
    first = decay_rows(my_heads(core, jnp.where(core == 0, fmine_ref[HALF:, :], fpeer_ref[HALF:, :])))
    mine, peer = mine_ref[...], peer_ref[...]
    chip = jnp.where(core == 0, mine, peer) + jnp.where(core == 0, peer, mine) * first
    out_ref[:, PIECE:, :] = chip.reshape(CHIPS, PIECE, STATE)
    acc = [jnp.zeros((1, STATE), f32)] * PIECE
    for k in range(CHIPS):
        keep = jnp.exp(in_ref[k, :, PIECE * STATE:])
        for r in range(PIECE):
            out_ref[k, r:r + 1, :] = acc[r]
            acc[r] = acc[r] * keep + in_ref[k, :, r * STATE:(r + 1) * STATE]


def scan_backward(dec_ref, in_ref, out_ref):
    acc = jnp.zeros((PIECE, STATE), f32)
    for k in range(CHIPS - 1, -1, -1):
        out_ref[k] = acc
        acc = acc * jnp.exp(dec_ref[k, :, PIECE * STATE:]) + in_ref[k, PIECE:, :]


def core_forward(got_ref, mine_ref, peer_ref, keep_ref, send_ref):
    core = place_of()[2]
    into = got_ref[:, :PIECE, :].reshape(HALF, STATE)
    first = decay_rows(my_heads(core, jnp.where(core == 0, mine_ref[HALF:, :], peer_ref[HALF:, :])))
    after = into * first + jnp.where(core == 0, mine_ref[:HALF, :], peer_ref[:HALF, :])
    keep_ref[...] = jnp.where(core == 0, into, after)
    send_ref[...] = jnp.where(core == 0, after, into)


def core_backward(got_ref, mine_ref, peer_ref, fmine_ref, fpeer_ref, keep_ref, send_ref):
    core = place_of()[2]
    after = got_ref[...].reshape(HALF, STATE)
    second = decay_rows(my_heads(core, jnp.where(core == 0, fpeer_ref[HALF:, :], fmine_ref[HALF:, :])))
    into = after * second + jnp.where(core == 0, peer_ref[...], mine_ref[...])
    keep_ref[...] = jnp.where(core == 0, into, after)
    send_ref[...] = jnp.where(core == 0, after, into)


def both_halves(core, keep, recv):
    low = jnp.where(core == 0, keep, recv)
    high = jnp.where(core == 0, recv, keep)
    return jnp.concatenate([low, high], axis=0).astype(bf16)


def intra_forward(rate_ref, dt_ref, x_ref, b_ref, c_ref, out_ref):
    dt = dt_ref[...].astype(f32)
    rate = rate_rows(rate_ref)
    rows, cols = row_sums(dt), column_sums(dt)
    xw = (x_ref[...].astype(f32) * spread(gate(dt * (2.0 * rate)))).astype(bf16)
    scores = mm(c_ref[...], b_ref[...], NT)
    i = lax.broadcasted_iota(jnp.int32, (TOK, TOK), 0)
    j = lax.broadcasted_iota(jnp.int32, (TOK, TOK), 1)
    for h in range(HEADS):
        lanes = slice(h * HEAD_DIM, (h + 1) * HEAD_DIM)
        gap = (rows[h:h + 1, :] - cols[:, h:h + 1]) * (rate_ref[h] * RATE_UNIT)
        mask = jnp.exp(jnp.where(i >= j, gap, -jnp.inf))
        out_ref[:, lanes] = mm((mask * scores).astype(bf16), xw[:, lanes], NN)
    out_ref[:, CH:] = spread(jnp.exp((before_first(dt) - rows) * rate))


def select_rows(core, y_at):
    row = lax.broadcasted_iota(jnp.int32, (CH // 2, CH), 0)
    lane = lax.broadcasted_iota(jnp.int32, (CH // 2, CH), 1)
    y = (y_at + row // 64) % NY
    z = (row // 8) % NZ
    return jnp.where(lane == ((z * NY + y) * 2 + core) * 8 + row % 8, 1.0, 0.0).astype(bf16)


def forward_out(keep_ref, recv_ref, c_ref, y_ref, out_ref, mine_ref, other_ref):
    _, y_at, core, _ = place_of()
    state = both_halves(core, keep_ref[...], recv_ref[...])
    out = (y_ref[:, :CH] + y_ref[:, CH:] * mm(c_ref[...], state, NT)).astype(bf16)
    out_ref[...] = out
    mine_ref[...] = mm(select_rows(core, y_at), out, NT).astype(bf16)
    other_ref[...] = mm(select_rows(1 - core, y_at), out, NT)


def partial_grad(rows_ref, peer_ref, g_ref, gp_ref, s0_ref, s1_ref, s2_ref, s3_ref):
    _, _, core, x_at = place_of()
    outs = (s0_ref, s1_ref, s2_ref, s3_ref)
    mine = rows_ref[...]
    peer = peer_ref[...].astype(bf16)
    for xr in range(NX):
        at = pl.multiple_of(((x_at + xr) % NX) * BLK, 128)
        tile = mm(mine, g_ref[:, pl.ds(at, BLK)], NN)
        tile = tile + mm(peer, gp_ref[:, pl.ds(at, BLK)].astype(bf16), NN)

        @pl.when(core == 0)
        def _():
            for yr in range(NY):
                outs[xr][yr] = tile[yr * 64:(yr + 1) * 64]

        @pl.when(core == 1)
        def _():
            for yr in range(NY):
                outs[yr][xr] = tile[yr * 64:(yr + 1) * 64]


def gradients(rate_ref, dt_ref, x_ref, b_ref, c_ref, gy_ref, keep_ref, recv_ref, after_ref, recv2_ref,
              gi_ref, gwr_ref, grd_ref):
    core = place_of()[2]
    dt = dt_ref[...].astype(f32)
    rate = rate_rows(rate_ref)
    rows, cols = row_sums(dt), column_sums(dt)
    gates = gate(dt * (2.0 * rate))
    w = spread(gates)
    wt = spread(gates * jnp.exp((rows - rows[:, TOK - 1:]) * rate))
    x = x_ref[...].astype(f32)
    xw, xt = (x * w).astype(bf16), (x * wt).astype(bf16)
    gy = gy_ref[...]
    gyd = (gy.astype(f32) * spread(jnp.exp((before_first(dt) - rows) * rate))).astype(bf16)
    b = b_ref[...]
    c = c_ref[...]
    scores = mm(b, c, NT)
    j = lax.broadcasted_iota(jnp.int32, (TOK, TOK), 0)
    i = lax.broadcasted_iota(jnp.int32, (TOK, TOK), 1)
    state = both_halves(core, keep_ref[...], recv_ref[...])
    adj = both_halves(core, after_ref[...], recv2_ref[...])
    inter = wt * mm(b, adj, NT)
    pairs = jnp.zeros((TOK, TOK), f32)
    for h in range(HEADS):
        lanes = slice(h * HEAD_DIM, (h + 1) * HEAD_DIM)
        gap = (cols[:, h:h + 1] - rows[h:h + 1, :]) * (rate_ref[h] * RATE_UNIT)
        mask = jnp.exp(jnp.where(i >= j, gap, -jnp.inf))
        intra = mm((mask * scores).astype(bf16), gy[:, lanes], NN)
        gi_ref[:, lanes] = (w[:, lanes] * intra + inter[:, lanes]).astype(bf16)
        pairs = pairs + mask * mm(xw[:, lanes], gy[:, lanes], NT)
    pairs = pairs.astype(bf16)
    grd_ref[...] = (mm(pairs, b, TN) + mm(gyd, state, NN)).astype(bf16)
    gwr_ref[...] = (mm(pairs, c, NN) + mm(xt, adj, NN)).astype(bf16)


def place(r0_ref, r1_ref, r2_ref, r3_ref, out_ref):
    x_at = place_of()[3]
    for k, ref in enumerate((r0_ref, r1_ref, r2_ref, r3_ref)):
        at = pl.multiple_of(((x_at + NX - k) % NX) * BLK, 128)
        out_ref[:, pl.ds(at, BLK)] = ref[...]


class Fetched:
    def __init__(self, copy, buffer):
        self.copy, self.buffer, self.here = copy, buffer, False

    def wait(self):
        if not self.here:
            self.copy.wait()
            self.here = True

    def __getitem__(self, at):
        self.wait()
        return self.buffer[at]


def call(body, outs, fetch, *args, us=1):
    shapes = [jax.ShapeDtypeStruct(s, d) for s, d in outs]
    moved = sum(a.size * a.dtype.itemsize for a in args) + sum(s.size * s.dtype.itemsize for s in shapes)
    scratch = [(pltpu.SMEM if a.ndim == 1 else pltpu.VMEM)(a.shape, a.dtype) for a in args[:fetch]]
    if fetch:
        scratch.append(pltpu.SemaphoreType.DMA((fetch,)))

    def kernel(*refs):
        left = refs[len(args) + len(outs):]
        held = [Fetched(pltpu.make_async_copy(refs[n], left[n], left[fetch].at[n]), left[n]) for n in range(fetch)]
        for one in held:
            one.copy.start()
        body(*held, *refs[fetch:len(args) + len(outs)])
        for one in held:
            one.wait()

    got = pl.pallas_call(
        kernel,
        out_shape=shapes,
        in_specs=[pl.BlockSpec(memory_space=pltpu.HBM)] * fetch
        + [pl.BlockSpec(memory_space=pltpu.VMEM)] * (len(args) - fetch),
        out_specs=[pl.BlockSpec(memory_space=pltpu.VMEM)] * len(shapes),
        scratch_shapes=scratch,
        cost_estimate=pl.CostEstimate(flops=us * 1_000_000_000, bytes_accessed=moved, transcendentals=0),
        compiler_params=pltpu.CompilerParams(vmem_limit_bytes=(12 << 20) if fetch else (4 << 20)),
        name=body.__name__,
    )(*[pltpu.with_memory_space_constraint(a, pltpu.HBM) if n < fetch else a for n, a in enumerate(args)])
    return got if len(got) > 1 else got[0]


def shards(inputs, write_vecs, read_vecs, dt_code, a_rate, w_out, grad_out):
    x, b, c, dt, g = inputs[0], write_vecs[0], read_vecs[0], dt_code[0], grad_out[0]
    chips = [[q * 2 + core for q in range(CHIPS)] for core in range(2)]
    depth = [[(z * NY + y) * 2 + core for z in range(NZ)] for y in range(NY) for core in range(2)]

    def over(v, groups):
        return lax.all_to_all(v, "seq", 0, 0, axis_index_groups=groups, tiled=True)

    half = ((HALF, STATE), f32)
    tokens, narrow = ((TOK, CH), bf16), ((TOK, STATE), bf16)
    both = ((HALF + 8, STATE), f32)
    mine, send = call(local_forward, [both, both], 4, a_rate, dt, x, b, us=2)
    peer = permute(send, swap_core)
    chip = call(chip_forward, [((CHIPS, 1, (PIECE + 1) * STATE), f32)], 0, mine, peer)
    pieces = over(chip, chips)

    g2 = lax.optimization_barrier((g, chip))[0]
    bmine, bsend, gy, g_wide = call(local_backward, [half, half, tokens, ((TOK, D), f32)], 5,
                                    a_rate, dt, c, g2, w_out, us=4)
    bpeer = permute(bsend, swap_core)
    pieces, bpeer, g_wide = lax.optimization_barrier((pieces, bpeer, g_wide))
    g_peer = permute(g_wide, swap_core)
    back = call(scan_forward, [((CHIPS, 2 * PIECE, STATE), f32)], 0, pieces, bmine, bpeer, mine, peer)
    got = over(back, chips)
    x2 = lax.optimization_barrier((x, back))[0]
    y_in = call(intra_forward, [((TOK, 2 * CH), f32)], 5, a_rate, dt, x2, b, c, us=3)
    got, y_in = lax.optimization_barrier((got, y_in))
    keep, send = call(core_forward, [half, half], 0, got, mine, peer)
    recv = permute(send, swap_core)
    out, rows, send = call(
        forward_out, [tokens, ((HALF, TOK), bf16), ((HALF, TOK), f32)], 0, keep, recv, c, y_in, us=2)
    s = call(partial_grad, [((NY, 64, BLK), f32)] * 4, 0, rows, permute(send, swap_core), g, g_peer, us=4)

    got2, pieces2 = lax.optimization_barrier((got, pieces, s[1]))[:2]
    back = over(call(scan_backward, [((CHIPS, PIECE, STATE), f32)], 0, pieces2, got2), chips)
    s1, s2, s3 = permute(s[1], first_axis(1)), permute(s[2], first_axis(2)), permute(s[3], first_axis(3))
    s1, s2, s3, back = lax.optimization_barrier((s1, s2, s3, back))
    s = s[0] + s2 + s1 + s3
    after, send = call(core_backward, [half, half], 0, back, bmine, bpeer, mine, peer)
    recv2 = permute(send, swap_core)
    s = s[0] + permute(s[2], second_axis(2)) + permute(s[1], second_axis(1)) + permute(s[3], second_axis(3))
    s = over(s.reshape(NZ, 8, BLK), depth)
    gi, gwr, grd = call(gradients, [tokens, narrow, narrow], 5, a_rate, dt, x2, b, c, gy, keep, recv, after, recv2, us=5)
    s, gi = lax.optimization_barrier((s, gi))
    s = jnp.sum(s, axis=0)
    grad_w_out = call(place, [((8, D), f32)], 0, s, permute(s, x_axis(1)), permute(s, x_axis(2)), permute(s, x_axis(3)))
    return out[None], gi[None], gwr[None], grd[None], grad_w_out


def solution(mesh):
    rows = P("dp", "seq", None)
    return jax.shard_map(
        shards,
        mesh=mesh,
        in_specs=(rows, rows, rows, P("dp", None, "seq"), P(), P(), rows),
        out_specs=(rows, rows, rows, rows, P("seq", None)),
        check_vma=False,
    )
```

```python
import jax
import jax.numpy as jnp
from jax import lax
from jax.experimental import pallas as pl
from jax.experimental.pallas import tpu as pltpu
from jax.sharding import PartitionSpec as P

HEAD_DIM = 64
STATE = 128
HEADS = 8
TOK = 256
CH = HEADS * HEAD_DIM
D = 2560
NX, NY, NZ = 4, 4, 8
CHIPS = NY * NZ
HALF = CH // 2
PIECE = HALF // CHIPS
BLK = D // NX
BOTH = ("seq", "dp")

f32, bf16 = jnp.float32, jnp.bfloat16
RATE_UNIT = 1.0 / (8.0 * TOK * 64)
HI = lax.Precision.HIGHEST
NT = (((1,), (1,)), ((), ()))
TN = (((0,), (0,)), ((), ()))
NN = (((1,), (0,)), ((), ()))


def mm(a, b, dims):
    return lax.dot_general(a, b, dims, preferred_element_type=f32)


def permute(v, target):
    pairs = []
    for z in range(NZ):
        for y in range(NY):
            for c in range(2):
                for x in range(NX):
                    tz, ty, tc, tx = target(z, y, c, x)
                    src = ((z * NY + y) * 2 + c) * NX + x
                    dst = ((tz * NY + ty) * 2 + tc) * NX + tx
                    pairs.append((src, dst))
    return lax.ppermute(v, BOTH, pairs)


def swap_core(z, y, c, x):
    return z, y, 1 - c, x


def first_axis(k):
    return lambda z, y, c, x: (z, y, c, (x + k) % NX) if c == 0 else (z, (y + k) % NY, c, x)


def second_axis(k):
    return lambda z, y, c, x: (z, (y + k) % NY, c, x) if c == 0 else (z, y, c, (x + k) % NX)


def x_axis(k):
    return lambda z, y, c, x: (z, y, c, (x + k) % NX)


def place_of():
    at = lax.axis_index("seq")
    return at >> 3, (at >> 1) & 3, at & 1, lax.axis_index("dp")


def rate_rows(rate_ref):
    head = lax.broadcasted_iota(jnp.int32, (HEADS, 1), 0)
    rates = jnp.zeros((HEADS, 1), f32)
    for h in range(HEADS):
        rates = jnp.where(head == h, rate_ref[h] * RATE_UNIT, rates)
    return rates


def signed_tri():
    t = lax.broadcasted_iota(jnp.int32, (TOK, TOK), 0)
    s = lax.broadcasted_iota(jnp.int32, (TOK, TOK), 1)
    half = TOK // 2
    plus = (s >= half) & (s <= t)
    minus = (s < half) & (s > t)
    return jnp.where(plus, 1.0, jnp.where(minus, -1.0, 0.0)).astype(f32)


def row_sums(dt):
    return lax.dot_general(dt, signed_tri(), NT, precision=HI, preferred_element_type=f32)


def column_sums(dt):
    return lax.dot_general(signed_tri(), dt, NT, precision=HI, preferred_element_type=f32)


def before_first(dt):
    return -jnp.sum(dt[:, : TOK // 2], axis=1, keepdims=True)


def spread(rows):
    head = lax.broadcasted_iota(jnp.int32, (HEADS, CH), 0)
    lane = lax.broadcasted_iota(jnp.int32, (HEADS, CH), 1) // HEAD_DIM
    pick = jnp.where(head == lane, 1.0, 0.0).astype(f32)
    return lax.dot_general(rows, pick, TN, precision=HI, preferred_element_type=f32)


def gate(v):
    s = 1.0 - v * (1.0 / 8.0)
    for n in (7.0, 6.0, 5.0, 4.0, 3.0, 2.0):
        s = 1.0 - v * (1.0 / n) * s
    return jnp.sqrt(jnp.where(v < 0.25, v * s, 1.0 - jnp.exp(-v)))


def local_forward(rate_ref, dt_ref, x_ref, b_ref, mine_ref, send_ref):
    core = place_of()[2]
    dt = dt_ref[...].astype(f32)
    rate = rate_rows(rate_ref)
    cum = row_sums(dt)
    tail = jnp.exp((cum - cum[:, TOK - 1:]) * rate)
    xt = (x_ref[...].astype(f32) * spread(gate(dt * (2.0 * rate)) * tail)).astype(bf16)
    own = mm(xt, b_ref[...], TN)
    tot = jnp.broadcast_to(-(jnp.sum(dt, axis=1, keepdims=True) * rate), (HEADS, STATE))
    mine_ref[HALF:, :] = tot
    send_ref[HALF:, :] = tot

    @pl.when(core == 0)
    def _():
        mine_ref[:HALF, :] = own[:HALF]
        send_ref[:HALF, :] = own[HALF:]

    @pl.when(core == 1)
    def _():
        mine_ref[:HALF, :] = own[HALF:]
        send_ref[:HALF, :] = own[:HALF]


def local_backward(rate_ref, dt_ref, c_ref, g_ref, w_ref, mine_ref, send_ref, gy_ref, wide_ref):
    core = place_of()[2]
    dt = dt_ref[...].astype(f32)
    decay = spread(jnp.exp((before_first(dt) - row_sums(dt)) * rate_rows(rate_ref)))
    g = g_ref[...]
    wide_ref[...] = g.astype(f32)
    gy = mm(g, w_ref[...], NT).astype(bf16)
    gy_ref[...] = gy
    adj = mm((gy.astype(f32) * decay).astype(bf16), c_ref[...], TN)

    @pl.when(core == 0)
    def _():
        mine_ref[...] = adj[:HALF]
        send_ref[...] = adj[HALF:]

    @pl.when(core == 1)
    def _():
        mine_ref[...] = adj[HALF:]
        send_ref[...] = adj[:HALF]


def my_heads(core, tots):
    return jnp.where(core == 0, tots[:HEADS // 2], tots[HEADS // 2:])


def decay_rows(tots):
    rows = jnp.exp(tots)
    return jnp.broadcast_to(rows[:, None, :], (HEADS // 2, HEAD_DIM, STATE)).reshape(HALF, STATE)


def chip_forward(mine_ref, peer_ref, out_ref):
    core = place_of()[2]
    own = my_heads(core, mine_ref[HALF:, :])
    other = my_heads(core, peer_ref[HALF:, :])
    mine, peer = mine_ref[:HALF, :], peer_ref[:HALF, :]
    second = decay_rows(jnp.where(core == 0, other, own))
    chip = jnp.where(core == 0, mine, peer) * second + jnp.where(core == 0, peer, mine)
    rows = chip.reshape(CHIPS, PIECE, STATE)
    for r in range(PIECE):
        out_ref[:, 0, r * STATE:(r + 1) * STATE] = rows[:, r, :]
    tots = jnp.broadcast_to((own + other)[:, None, :], (HEADS // 2, CHIPS // (HEADS // 2), STATE))
    out_ref[:, 0, PIECE * STATE:] = tots.reshape(CHIPS, STATE)


def scan_forward(in_ref, mine_ref, peer_ref, fmine_ref, fpeer_ref, out_ref):
    core = place_of()[2]
    first = decay_rows(my_heads(core, jnp.where(core == 0, fmine_ref[HALF:, :], fpeer_ref[HALF:, :])))
    mine, peer = mine_ref[...], peer_ref[...]
    chip = jnp.where(core == 0, mine, peer) + jnp.where(core == 0, peer, mine) * first
    out_ref[:, PIECE:, :] = chip.reshape(CHIPS, PIECE, STATE)
    acc = [jnp.zeros((1, STATE), f32)] * PIECE
    for k in range(CHIPS):
        keep = jnp.exp(in_ref[k, :, PIECE * STATE:])
        for r in range(PIECE):
            out_ref[k, r:r + 1, :] = acc[r]
            acc[r] = acc[r] * keep + in_ref[k, :, r * STATE:(r + 1) * STATE]


def scan_backward(dec_ref, in_ref, out_ref):
    acc = jnp.zeros((PIECE, STATE), f32)
    for k in range(CHIPS - 1, -1, -1):
        out_ref[k] = acc
        acc = acc * jnp.exp(dec_ref[k, :, PIECE * STATE:]) + in_ref[k, PIECE:, :]


def core_forward(got_ref, mine_ref, peer_ref, keep_ref, send_ref):
    core = place_of()[2]
    into = got_ref[:, :PIECE, :].reshape(HALF, STATE)
    first = decay_rows(my_heads(core, jnp.where(core == 0, mine_ref[HALF:, :], peer_ref[HALF:, :])))
    after = into * first + jnp.where(core == 0, mine_ref[:HALF, :], peer_ref[:HALF, :])
    keep_ref[...] = jnp.where(core == 0, into, after)
    send_ref[...] = jnp.where(core == 0, after, into)


def core_backward(got_ref, mine_ref, peer_ref, fmine_ref, fpeer_ref, keep_ref, send_ref):
    core = place_of()[2]
    after = got_ref[...].reshape(HALF, STATE)
    second = decay_rows(my_heads(core, jnp.where(core == 0, fpeer_ref[HALF:, :], fmine_ref[HALF:, :])))
    into = after * second + jnp.where(core == 0, peer_ref[...], mine_ref[...])
    keep_ref[...] = jnp.where(core == 0, into, after)
    send_ref[...] = jnp.where(core == 0, after, into)


def both_halves(core, keep, recv):
    low = jnp.where(core == 0, keep, recv)
    high = jnp.where(core == 0, recv, keep)
    return jnp.concatenate([low, high], axis=0).astype(bf16)


def intra_forward(rate_ref, dt_ref, x_ref, b_ref, c_ref, out_ref):
    dt = dt_ref[...].astype(f32)
    rate = rate_rows(rate_ref)
    rows, cols = row_sums(dt), column_sums(dt)
    xw = (x_ref[...].astype(f32) * spread(gate(dt * (2.0 * rate)))).astype(bf16)
    scores = mm(c_ref[...], b_ref[...], NT)
    i = lax.broadcasted_iota(jnp.int32, (TOK, TOK), 0)
    j = lax.broadcasted_iota(jnp.int32, (TOK, TOK), 1)
    for h in range(HEADS):
        lanes = slice(h * HEAD_DIM, (h + 1) * HEAD_DIM)
        gap = (rows[h:h + 1, :] - cols[:, h:h + 1]) * (rate_ref[h] * RATE_UNIT)
        mask = jnp.exp(jnp.where(i >= j, gap, -jnp.inf))
        out_ref[:, lanes] = mm((mask * scores).astype(bf16), xw[:, lanes], NN)
    out_ref[:, CH:] = spread(jnp.exp((before_first(dt) - rows) * rate))


def select_rows(core, y_at):
    row = lax.broadcasted_iota(jnp.int32, (CH // 2, CH), 0)
    lane = lax.broadcasted_iota(jnp.int32, (CH // 2, CH), 1)
    y = (y_at + row // 64) % NY
    z = (row // 8) % NZ
    return jnp.where(lane == ((z * NY + y) * 2 + core) * 8 + row % 8, 1.0, 0.0).astype(bf16)


def forward_out(keep_ref, recv_ref, c_ref, y_ref, out_ref, mine_ref, other_ref):
    _, y_at, core, _ = place_of()
    state = both_halves(core, keep_ref[...], recv_ref[...])
    out = (y_ref[:, :CH] + y_ref[:, CH:] * mm(c_ref[...], state, NT)).astype(bf16)
    out_ref[...] = out
    mine_ref[...] = mm(select_rows(core, y_at), out, NT).astype(bf16)
    other_ref[...] = mm(select_rows(1 - core, y_at), out, NT)


def partial_grad(rows_ref, peer_ref, g_ref, gp_ref, s0_ref, s1_ref, s2_ref, s3_ref):
    _, _, core, x_at = place_of()
    outs = (s0_ref, s1_ref, s2_ref, s3_ref)
    mine = rows_ref[...]
    peer = peer_ref[...].astype(bf16)
    for xr in range(NX):
        at = pl.multiple_of(((x_at + xr) % NX) * BLK, 128)
        tile = mm(mine, g_ref[:, pl.ds(at, BLK)], NN)
        tile = tile + mm(peer, gp_ref[:, pl.ds(at, BLK)].astype(bf16), NN)

        @pl.when(core == 0)
        def _():
            for yr in range(NY):
                outs[xr][yr] = tile[yr * 64:(yr + 1) * 64]

        @pl.when(core == 1)
        def _():
            for yr in range(NY):
                outs[yr][xr] = tile[yr * 64:(yr + 1) * 64]


def gradients(rate_ref, dt_ref, x_ref, b_ref, c_ref, gy_ref, keep_ref, recv_ref, after_ref, recv2_ref,
              gi_ref, gwr_ref, grd_ref):
    core = place_of()[2]
    dt = dt_ref[...].astype(f32)
    rate = rate_rows(rate_ref)
    rows, cols = row_sums(dt), column_sums(dt)
    gates = gate(dt * (2.0 * rate))
    w = spread(gates)
    wt = spread(gates * jnp.exp((rows - rows[:, TOK - 1:]) * rate))
    x = x_ref[...].astype(f32)
    xw, xt = (x * w).astype(bf16), (x * wt).astype(bf16)
    gy = gy_ref[...]
    gyd = (gy.astype(f32) * spread(jnp.exp((before_first(dt) - rows) * rate))).astype(bf16)
    b = b_ref[...]
    c = c_ref[...]
    scores = mm(b, c, NT)
    j = lax.broadcasted_iota(jnp.int32, (TOK, TOK), 0)
    i = lax.broadcasted_iota(jnp.int32, (TOK, TOK), 1)
    state = both_halves(core, keep_ref[...], recv_ref[...])
    adj = both_halves(core, after_ref[...], recv2_ref[...])
    inter = wt * mm(b, adj, NT)
    pairs = jnp.zeros((TOK, TOK), f32)
    for h in range(HEADS):
        lanes = slice(h * HEAD_DIM, (h + 1) * HEAD_DIM)
        gap = (cols[:, h:h + 1] - rows[h:h + 1, :]) * (rate_ref[h] * RATE_UNIT)
        mask = jnp.exp(jnp.where(i >= j, gap, -jnp.inf))
        intra = mm((mask * scores).astype(bf16), gy[:, lanes], NN)
        gi_ref[:, lanes] = (w[:, lanes] * intra + inter[:, lanes]).astype(bf16)
        pairs = pairs + mask * mm(xw[:, lanes], gy[:, lanes], NT)
    pairs = pairs.astype(bf16)
    grd_ref[...] = (mm(pairs, b, TN) + mm(gyd, state, NN)).astype(bf16)
    gwr_ref[...] = (mm(pairs, c, NN) + mm(xt, adj, NN)).astype(bf16)


def place(r0_ref, r1_ref, r2_ref, r3_ref, out_ref):
    x_at = place_of()[3]
    for k, ref in enumerate((r0_ref, r1_ref, r2_ref, r3_ref)):
        at = pl.multiple_of(((x_at + NX - k) % NX) * BLK, 128)
        out_ref[:, pl.ds(at, BLK)] = ref[...]


class Fetched:
    def __init__(self, copy, buffer):
        self.copy, self.buffer, self.here = copy, buffer, False

    def wait(self):
        if not self.here:
            self.copy.wait()
            self.here = True

    def __getitem__(self, at):
        self.wait()
        return self.buffer[at]


def call(body, outs, fetch, *args, us=1, grant=None):
    shapes = [jax.ShapeDtypeStruct(s, d) for s, d in outs]
    moved = sum(a.size * a.dtype.itemsize for a in args) + sum(s.size * s.dtype.itemsize for s in shapes)
    scratch = [(pltpu.SMEM if a.ndim == 1 else pltpu.VMEM)(a.shape, a.dtype) for a in args[:fetch]]
    if fetch:
        scratch.append(pltpu.SemaphoreType.DMA((fetch,)))

    def kernel(*refs):
        left = refs[len(args) + len(outs):]
        held = [Fetched(pltpu.make_async_copy(refs[n], left[n], left[fetch].at[n]), left[n]) for n in range(fetch)]
        for one in held:
            one.copy.start()
        body(*held, *refs[fetch:len(args) + len(outs)])
        for one in held:
            one.wait()

    got = pl.pallas_call(
        kernel,
        out_shape=shapes,
        in_specs=[pl.BlockSpec(memory_space=pltpu.HBM)] * fetch
        + [pl.BlockSpec(memory_space=pltpu.VMEM)] * (len(args) - fetch),
        out_specs=[pl.BlockSpec(memory_space=pltpu.VMEM)] * len(shapes),
        scratch_shapes=scratch,
        cost_estimate=pl.CostEstimate(flops=us * 1_000_000_000, bytes_accessed=moved, transcendentals=0),
        compiler_params=pltpu.CompilerParams(vmem_limit_bytes=grant or (12 << 20 if fetch else 4 << 20)),
        name=body.__name__,
    )(*[pltpu.with_memory_space_constraint(a, pltpu.HBM) if n < fetch else a for n, a in enumerate(args)])
    return got if len(got) > 1 else got[0]


def shards(inputs, write_vecs, read_vecs, dt_code, a_rate, w_out, grad_out):
    x, b, c, dt, g = inputs[0], write_vecs[0], read_vecs[0], dt_code[0], grad_out[0]
    chips = [[q * 2 + core for q in range(CHIPS)] for core in range(2)]
    depth = [[(z * NY + y) * 2 + core for z in range(NZ)] for y in range(NY) for core in range(2)]

    def over(v, groups):
        return lax.all_to_all(v, "seq", 0, 0, axis_index_groups=groups, tiled=True)

    half = ((HALF, STATE), f32)
    tokens, narrow = ((TOK, CH), bf16), ((TOK, STATE), bf16)
    both = ((HALF + 8, STATE), f32)
    mine, send = call(local_forward, [both, both], 4, a_rate, dt, x, b, us=2)
    peer = permute(send, swap_core)
    chip = call(chip_forward, [((CHIPS, 1, (PIECE + 1) * STATE), f32)], 0, mine, peer)
    pieces = over(chip, chips)

    g2 = lax.optimization_barrier((g, chip))[0]
    bmine, bsend, gy, g_wide = call(local_backward, [half, half, tokens, ((TOK, D), f32)], 5,
                                    a_rate, dt, c, g2, w_out, us=4, grant=54 << 20)
    bpeer = permute(bsend, swap_core)
    pieces, bpeer, g_wide = lax.optimization_barrier((pieces, bpeer, g_wide))
    g_peer = permute(g_wide, swap_core)
    back = call(scan_forward, [((CHIPS, 2 * PIECE, STATE), f32)], 0, pieces, bmine, bpeer, mine, peer)
    got = over(back, chips)
    x2 = lax.optimization_barrier((x, back))[0]
    y_in = call(intra_forward, [((TOK, 2 * CH), f32)], 5, a_rate, dt, x2, b, c, us=3)
    got, y_in = lax.optimization_barrier((got, y_in))
    keep, send = call(core_forward, [half, half], 0, got, mine, peer)
    recv = permute(send, swap_core)
    out, rows, send = call(
        forward_out, [tokens, ((HALF, TOK), bf16), ((HALF, TOK), f32)], 0, keep, recv, c, y_in, us=2)
    s = call(partial_grad, [((NY, 64, BLK), f32)] * 4, 0, rows, permute(send, swap_core), g, g_peer, us=4)

    got2, pieces2 = lax.optimization_barrier((got, pieces, s[1]))[:2]
    back = over(call(scan_backward, [((CHIPS, PIECE, STATE), f32)], 0, pieces2, got2), chips)
    s1, s2, s3 = permute(s[1], first_axis(1)), permute(s[2], first_axis(2)), permute(s[3], first_axis(3))
    s1, s2, s3, back = lax.optimization_barrier((s1, s2, s3, back))
    s = s[0] + s2 + s1 + s3
    after, send = call(core_backward, [half, half], 0, back, bmine, bpeer, mine, peer)
    recv2 = permute(send, swap_core)
    s = s[0] + permute(s[2], second_axis(2)) + permute(s[1], second_axis(1)) + permute(s[3], second_axis(3))
    s = over(s.reshape(NZ, 8, BLK), depth)
    gi, gwr, grd = call(gradients, [tokens, narrow, narrow], 5, a_rate, dt, x2, b, c, gy, keep, recv, after, recv2, us=5)
    s, gi = lax.optimization_barrier((s, gi))
    s = jnp.sum(s, axis=0)
    grad_w_out = call(place, [((8, D), f32)], 0, s, permute(s, x_axis(1)), permute(s, x_axis(2)), permute(s, x_axis(3)))
    return out[None], gi[None], gwr[None], grd[None], grad_w_out


def solution(mesh):
    rows = P("dp", "seq", None)
    return jax.shard_map(
        shards,
        mesh=mesh,
        in_specs=(rows, rows, rows, P("dp", None, "seq"), P(), P(), rows),
        out_specs=(rows, rows, rows, rows, P("seq", None)),
        check_vma=False,
    )
```
